128 devices in a mesh: lat: 16 (over z, y), lon: 8 (over x, core).
Axes of the slice: x: 4, y: 4, z: 4, core: 2. Of those that a mesh axis runs over, the one named last changes fastest.
Arguments:
- encoder_features: bfloat16 [512, 256, 128], P('lat', 'lon'), may hold values from -6 to 6
- noise: bfloat16 [512, 256, 128], P('lat', 'lon'), may hold values from -6 to 6
- patch_cols: int32 [16, 32], P('lat'), may hold values from 0 to 255, as said below
- timesteps: int32 [16, 32], P('lat'), may hold values from 0 to 31
- w_conv: bfloat16 [1152, 128], replicated, may hold values from -0.1875 to 0.1875
- w_down: bfloat16 [512, 256], replicated, may hold values from -0.25 to 0.25
- w_up: bfloat16 [256, 512], replicated, may hold values from -0.375 to 0.375
- w_out: bfloat16 [128, 128], replicated, may hold values from -0.5 to 0.5
Outputs:
- feature_grad: float32 [512, 256, 128], P('lat', 'lon')
- grad_conv: float32 [1152, 128], replicated
- grad_down: float32 [512, 256], replicated
- grad_up: float32 [256, 512], replicated
- grad_out: float32 [128, 128], replicated
- loss_value: float32 [], replicated
The draws below stay inside these ranges and needn't reach their ends.
Inputs may be any that keep to these rules, and one draw needn't show every extreme that they name: `patch_cols`: in each band at most 12 patches start in one device's block of 32 longitude cells, and exactly 12 start in one block.
All inputs are finite; a program needn't handle non-finite values.
Results may differ from the reference program's by a relative error of at most 0.009.
Values may be sent and summed in bfloat16 or wider, within the bound.
No kernel may reach another device: no remote copies, remote signals or barrier semaphores. Data moves between devices by JAX's collectives and lax.ppermute only.
A program may use at most 64 MiB of HBM per device.

```python
import math
import jax
import jax.numpy as jnp
from jax import lax

C = 128
PATCH = 32
NSTEPS = 32
CLON = 32
NLAT = 512
NLON = 256
NPB = 32
PMAX = 12
N_LAT = 16
N_LON = 8


def draw_patch_cols(key, part):
    key_busy = jax.random.fold_in(key, 11)
    key_offset = jax.random.fold_in(key, 12)
    busiest = jax.random.randint(key_busy, (N_LAT, 1), 0, N_LON)
    slots = jnp.arange(NPB, dtype=jnp.int32)[None, :]
    others = (busiest + 1 + (slots - PMAX) % (N_LON - 1)) % N_LON
    owners = jnp.where(slots < PMAX, busiest, others)
    offsets = jax.random.randint(key_offset, (N_LAT, NPB), 0, CLON)
    return (owners * CLON + offsets).astype(jnp.int32)


def touch_ends(result, stream_key, low, largest):
    longest = result.shape.index(max(result.shape))
    spots = []
    for shift in (0, 1):
        where = [jax.random.randint(jax.random.fold_in(stream_key, axis), (), 0, length) for axis, length in enumerate(result.shape)]
        where[longest] = (where[longest] + shift) % result.shape[longest]
        spots.append(tuple(where))
    return result.at[spots[0]].set(low).at[spots[1]].set(largest)


def level_of(rng, shape, cuts, smallest, high):
    def one(axis_at, parts):
        steps = jax.random.uniform(jax.random.fold_in(jax.random.fold_in(rng, 6), axis_at), (parts,), jnp.float32, smallest / len(cuts), high / len(cuts))
        return jnp.repeat(jnp.exp(steps), shape[axis_at] // parts).reshape((-1,) + (1,) * (len(shape) - axis_at - 1))

    gain = one(*cuts[0])
    for cut in cuts[1:]:
        gain = gain * one(*cut)
    return gain


def scatter_about(rng, shape, width, most, split=(), kind=jnp.bfloat16):
    array = width * jax.random.normal(rng, shape, jnp.float32)
    if split:
        array = array * level_of(rng, shape, split, -0.22, 0.18)
    return jnp.clip(array, -most, most).astype(kind)


def setup_inputs(seed: int = 0) -> dict:
    splits = jax.random.split(jax.random.key(seed), 9)
    return {
        "encoder_features": scatter_about(splits[0], (NLAT, NLON, C), 1.0, 6.0, ((0, 16), (1, 8))),
        "noise": scatter_about(splits[1], (NLAT, NLON, C), 1.0, 6.0, ((0, 16), (1, 8))),
        "patch_cols": draw_patch_cols(jax.random.fold_in(splits[8], 71), 0),
        "timesteps": touch_ends(jax.random.randint(splits[3], (N_LAT, NPB), 0, NSTEPS), jax.random.fold_in(splits[3], 1), 0, NSTEPS - 1).astype(jnp.int32),
        "w_conv": scatter_about(splits[4], (9 * C, C), (9 * C) ** -0.5, 0.1875),
        "w_down": scatter_about(splits[5], (4 * C, 2 * C), (4 * C) ** -0.5, 0.25),
        "w_up": scatter_about(splits[6], (2 * C, 4 * C), (2 * C) ** -0.5, 0.375),
        "w_out": scatter_about(splits[7], (C, C), C ** -0.5, 0.5),
    }


sigma_low = 0.02
sigma_high = 20.0

def sigma_of(levels):
    return sigma_low * jnp.exp(levels.astype(jnp.float32) / (NSTEPS - 1) * math.log(sigma_high / sigma_low))

def patch_loss(feat, noise_patch, sigma, w_conv, w_down, w_up, w_out):
    side = feat.shape[0]
    chans = feat.shape[2]
    scale_in = 1.0 / jnp.sqrt(1.0 + sigma * sigma)
    hidden = (scale_in * (feat + sigma * noise_patch.astype(jnp.float32))).astype(jnp.bfloat16)
    padded = jnp.pad(hidden, ((1, 1), (1, 1), (0, 0)))
    stacked = jnp.concatenate([padded[row_off:row_off + side, col_off:col_off + side] for row_off in range(3) for col_off in range(3)], axis=-1).reshape(side * side, 9 * chans)
    first = jax.nn.silu(jnp.dot(stacked, w_conv, preferred_element_type=jnp.float32)).astype(jnp.bfloat16)
    coarse_in = first.reshape(side // 2, 2, side // 2, 2, chans).transpose(0, 2, 1, 3, 4).reshape(side * side // 4, 4 * chans)
    coarse = jax.nn.silu(jnp.dot(coarse_in, w_down, preferred_element_type=jnp.float32)).astype(jnp.bfloat16)
    upward = jnp.dot(coarse, w_up, preferred_element_type=jnp.float32).reshape(side // 2, side // 2, 2, 2, chans).transpose(0, 2, 1, 3, 4).reshape(side * side, chans)
    merged = (first.astype(jnp.float32) + upward).astype(jnp.bfloat16)
    predicted = jnp.dot(merged, w_out, preferred_element_type=jnp.float32)
    error = predicted - noise_patch.reshape(side * side, chans).astype(jnp.float32)
    return jnp.sum(error * error) / (2.0 * chans)

def patch_grads(window_feat, window_noise, start, sigma, weights, live):
    side = window_feat.shape[0]
    feat = lax.dynamic_slice_in_dim(window_feat, start, side, 1).astype(jnp.float32)
    noise_patch = lax.dynamic_slice_in_dim(window_noise, start, side, 1)

    def local_loss(feat_in, conv_in, down_in, up_in, out_in):
        return patch_loss(feat_in, noise_patch, sigma, conv_in, down_in, up_in, out_in)
    value, pull = jax.vjp(local_loss, feat, *weights)
    return (value * live, pull(live))

def reference(encoder_features, noise, patch_cols, timesteps, w_conv, w_down, w_up, w_out):
    weights = (w_conv, w_down, w_up, w_out)
    side = PATCH
    chans = encoder_features.shape[2]

    def one_band(totals, band_index):
        feat_band = lax.dynamic_slice_in_dim(encoder_features, band_index * side, side, 0)
        noise_band = lax.dynamic_slice_in_dim(noise, band_index * side, side, 0)
        feat_ext = jnp.concatenate([feat_band, feat_band[:, :side]], axis=1)
        noise_ext = jnp.concatenate([noise_band, noise_band[:, :side]], axis=1)
        starts = lax.dynamic_index_in_dim(patch_cols, band_index, 0, keepdims=False)
        sigmas = sigma_of(lax.dynamic_index_in_dim(timesteps, band_index, 0, keepdims=False))

        def one_patch(inner, slot):
            grad_ext, sums = inner
            start = starts[slot]
            value, grads = patch_grads(feat_ext, noise_ext, start, sigmas[slot], weights, jnp.ones((), jnp.float32))
            current = lax.dynamic_slice_in_dim(grad_ext, start, side, 1)
            grad_ext = lax.dynamic_update_slice_in_dim(grad_ext, current + grads[0], start, 1)
            sums = tuple((total + part.astype(jnp.float32) for total, part in zip(sums[:4], grads[1:]))) + (sums[4] + value,)
            return ((grad_ext, sums), None)
        empty = jnp.zeros((side, NLON + side, chans), jnp.float32)
        (grad_ext, totals), unused = lax.scan(one_patch, (empty, totals), jnp.arange(NPB, dtype=jnp.int32))
        folded = grad_ext[:, :NLON].at[:, :side].add(grad_ext[:, NLON:])
        return (totals, folded)
    init = tuple((jnp.zeros(w.shape, jnp.float32) for w in weights)) + (jnp.zeros((), jnp.float32),)
    totals, band_grads = lax.scan(one_band, init, jnp.arange(N_LAT, dtype=jnp.int32))
    feature_grad = band_grads.reshape(NLAT, NLON, chans)
    loss_value = totals[4] / (N_LAT * NPB * side * side)
    return (feature_grad, totals[0], totals[1], totals[2], totals[3], loss_value)
```

```python
import math

import jax
import jax.numpy as jnp
from jax import lax
from jax.experimental import pallas as pl
from jax.experimental.pallas import tpu as pltpu
from jax.sharding import PartitionSpec as P

NSTEPS = 32
PMAX = 12
SIDE = 32
HALF = 16
C = 128
CELLS = SIDE * HALF
CHUNK = 32
NDEV = 128

sigma_low = 0.02
sigma_high = 20.0

bf16 = jnp.bfloat16
f32 = jnp.float32


def shifted(block, axis, distance):
    devices = range(lax.axis_size(axis))
    route = [((i - distance) % len(devices), i) for i in devices]
    return lax.ppermute(block, axis, route)


def sigma_of(levels):
    return sigma_low * jnp.exp(
        levels.astype(jnp.float32) / (NSTEPS - 1) * math.log(sigma_high / sigma_low)
    )


def dot(a, b):
    return jnp.dot(a, b, preferred_element_type=f32)


def dot_t(a, b):
    return lax.dot_general(a, b, (((0,), (0,)), ((), ())), preferred_element_type=f32)


def pack_rows(block):
    rows, cols, chans = block.shape
    return block.reshape(rows // 2, 2, cols, chans).transpose(2, 0, 1, 3).reshape(
        cols, rows // 2, 2 * chans
    )


def unpack_rows(block):
    cols, half, lanes = block.shape
    return block.reshape(cols, half, 2, lanes // 2).transpose(1, 2, 0, 3).reshape(
        2 * half, cols, lanes // 2
    )


def fill_slots(slots, value):
    row = lax.broadcasted_iota(jnp.int32, (CELLS, C), 0) % HALF
    even = value[:, :C]
    odd = value[:, C:]
    above = jnp.where(row == 0, 0.0, pltpu.roll(odd, 1, 0))
    below = jnp.where(row == HALF - 1, 0.0, pltpu.roll(even, CELLS - 1, 0))
    slots[1 : SIDE + 1, :, 0:C] = above.astype(bf16).reshape(SIDE, HALF, C)
    slots[1 : SIDE + 1, :, C : 3 * C] = value.astype(bf16).reshape(SIDE, HALF, 2 * C)
    slots[1 : SIDE + 1, :, 3 * C : 4 * C] = below.astype(bf16).reshape(SIDE, HALF, C)


def zero_edges(slots):
    slots[0] = jnp.zeros((HALF, 4 * C), bf16)
    slots[SIDE + 1] = jnp.zeros((HALF, 4 * C), bf16)


def taps(slots):
    return jnp.concatenate(
        [slots[d : d + SIDE].reshape(CELLS, 4 * C) for d in range(3)], axis=-1
    )


def patch_kernel(
    count, starts, alphas, betas,
    feat, noise, w_in, w_dn, w_dn_t, w_u, w_u_t, w_o, w_o_t,
    dpre_out, grads_out,
    slots, first, slope, g_conv, g_down, g_up, g_out, loss,
):
    g_conv[...] = jnp.zeros_like(g_conv)
    g_down[...] = jnp.zeros_like(g_down)
    g_up[...] = jnp.zeros_like(g_up)
    g_out[...] = jnp.zeros_like(g_out)
    loss[...] = jnp.zeros_like(loss)
    zero_edges(slots)

    def one_patch(k, carry):
        start = starts[k]
        f = feat[pl.ds(start, SIDE)].reshape(CELLS, 2 * C).astype(f32)
        e = noise[pl.ds(start, SIDE)].reshape(CELLS, 2 * C).astype(f32)
        fill_slots(slots, alphas[k] * f + betas[k] * e)
        pre = dot(taps(slots), w_in[...])
        sig = 0.5 * jnp.tanh(0.5 * pre) + 0.5
        act = pre * sig
        slope[...] = (sig + act * (1.0 - sig)).reshape(SLOPE)
        first[...] = act.astype(bf16).reshape(SLOPE)
        cells = jnp.concatenate([first[:, b].reshape(256, 256) for b in range(2)], axis=-1)
        pre2 = dot(cells, w_dn[...])
        sig2 = 0.5 * jnp.tanh(0.5 * pre2) + 0.5
        act2 = pre2 * sig2
        slope2 = sig2 + act2 * (1.0 - sig2)
        coarse = act2.astype(bf16)
        up = dot(coarse, w_u[...])
        ep = noise.at[pl.ds(start, SIDE)]
        merged = []
        dmerged = []
        derr = []
        for b in range(2):
            m = (first[:, b].reshape(256, 256).astype(f32) + up[:, 256 * b : 256 * b + 256]).astype(bf16)
            eps = ep[...].reshape(HALF, 2, HALF, 2 * C)[:, b].reshape(256, 256).astype(f32)
            err = dot(m, w_o[...]) - eps
            loss[...] += jnp.sum((err * err).reshape(32, 8, 256), axis=0)
            d = (err * (1.0 / C)).astype(bf16)
            merged.append(m)
            derr.append(d)
            dmerged.append(dot(d, w_o_t[...]).astype(bf16))
        g_out[...] += dot_t(jnp.concatenate(merged, axis=0), jnp.concatenate(derr, axis=0))
        dm = jnp.concatenate(dmerged, axis=-1)
        g_up[...] += dot_t(coarse, dm)
        dpre2 = (dot(dm, w_u_t[...]) * slope2).astype(bf16)
        g_down[...] += dot_t(dpre2, cells)
        dcells = dot(dpre2, w_dn_t[...])
        for b in range(2):
            df = dmerged[b].astype(f32) + dcells[:, 256 * b : 256 * b + 256]
            dp = df * slope[:, b].reshape(256, 256)
            first[:, b] = dp.astype(bf16).reshape(HALF, HALF, 2 * C)
        dpre = first[...].reshape(CELLS, 2 * C)
        dpre_out[k] = dpre
        g_conv[...] += dot_t(dpre, taps(slots))
        return carry

    lax.fori_loop(0, count[0], one_patch, 0)

    for i in range(3):
        for j in range(3):
            block = g_conv[0:C, pl.ds((4 * j + i) * C, C)] + g_conv[C:, pl.ds((4 * j + i + 1) * C, C)]
            grads_out[pl.ds((3 * i + j) * C, C)] = block.T.astype(bf16)
    base = 9 * C
    for a in range(2):
        for b in range(2):
            for h in range(2):
                block = g_down[h * C : h * C + C, (2 * b + a) * C : (2 * b + a + 1) * C]
                grads_out[pl.ds(base + ((2 * a + b) * 2 + h) * C, C)] = block.T.astype(bf16)
    base = 17 * C
    for a in range(2):
        for b in range(2):
            for h in range(2):
                block = g_up[h * C : h * C + C, (2 * b + a) * C : (2 * b + a + 1) * C]
                grads_out[pl.ds(base + ((2 * a + b) * 2 + h) * C, C)] = block.astype(bf16)
    base = 25 * C
    grads_out[pl.ds(base, C)] = (g_out[0:C, 0:C] + g_out[C:, C:]).astype(bf16)
    base = 26 * C
    part = jnp.sum(loss[:, 0:C] + loss[:, C:], axis=0, keepdims=True)
    high = part.astype(bf16)
    low = (part - high.astype(f32)).astype(bf16)
    row = lax.broadcasted_iota(jnp.int32, (C, C), 0)
    grads_out[pl.ds(base, C)] = jnp.where(
        row == 0, high.astype(f32), jnp.where(row == 1, low.astype(f32), 0.0)
    ).astype(bf16)
    grads_out[pl.ds(27 * C, 5 * C)] = jnp.zeros((5 * C, C), bf16)


SLOPE = (HALF, 2, HALF, 2 * C)


def input_kernel(count, starts, alphas, dpre, w_back, out, slots):
    out[...] = jnp.zeros_like(out)
    zero_edges(slots)

    def one_patch(k, carry):
        fill_slots(slots, dpre[k].astype(f32))
        back = dot(taps(slots), w_back[...]) * alphas[k]
        window = out.at[pl.ds(starts[k], SIDE)]
        window[...] += back.reshape(SIDE, HALF, 2 * C)
        return carry

    lax.fori_loop(0, count[0], one_patch, 0)


def smem():
    return pl.BlockSpec(memory_space=pltpu.SMEM)


def vmem():
    return pl.BlockSpec(memory_space=pltpu.VMEM)


def run_patches(count, starts, alphas, betas, feat, noise, weights):
    return pl.pallas_call(
        patch_kernel,
        out_shape=(
            jax.ShapeDtypeStruct((PMAX, CELLS, 2 * C), bf16),
            jax.ShapeDtypeStruct((NDEV * CHUNK, C), bf16),
        ),
        in_specs=[smem()] * 4 + [vmem()] * 9,
        out_specs=(vmem(), vmem()),
        scratch_shapes=[
            pltpu.VMEM((SIDE + 2, HALF, 4 * C), bf16),
            pltpu.VMEM(SLOPE, bf16),
            pltpu.VMEM(SLOPE, f32),
            pltpu.VMEM((2 * C, 12 * C), f32),
            pltpu.VMEM((2 * C, 4 * C), f32),
            pltpu.VMEM((2 * C, 4 * C), f32),
            pltpu.VMEM((2 * C, 2 * C), f32),
            pltpu.VMEM((8, 2 * C), f32),
        ],
        compiler_params=pltpu.CompilerParams(vmem_limit_bytes=50 << 20),
        name="patches",
    )(count, starts, alphas, betas, feat, noise, *weights)


def run_inputs(count, starts, alphas, dpre, w_back):
    return pl.pallas_call(
        input_kernel,
        out_shape=jax.ShapeDtypeStruct((2 * SIDE, HALF, 2 * C), f32),
        in_specs=[smem()] * 3 + [vmem()] * 2,
        out_specs=vmem(),
        scratch_shapes=[pltpu.VMEM((SIDE + 2, HALF, 4 * C), bf16)],
        compiler_params=pltpu.CompilerParams(vmem_limit_bytes=50 << 20),
        name="inputs",
    )(count, starts, alphas, dpre, w_back)


def layout_weights(w_conv, w_down, w_up, w_out):
    zero = jnp.zeros((C, C), bf16)
    conv = w_conv.reshape(3, 3, C, C)

    def fwd(dc, s, a):
        return conv[s - a, dc] if 0 <= s - a < 3 else zero

    def back(dc, s, p):
        return conv[p + 2 - s, 2 - dc].T if 0 <= p + 2 - s < 3 else zero

    def grid(block):
        return jnp.concatenate(
            [
                jnp.concatenate([block(dc, s, a) for a in range(2)], axis=1)
                for dc in range(3)
                for s in range(4)
            ],
            axis=0,
        )

    down = w_down.reshape(2, 2, C, 2 * C).transpose(1, 0, 2, 3).reshape(4 * C, 2 * C)
    up = w_up.reshape(2 * C, 2, 2, C).transpose(0, 2, 1, 3).reshape(2 * C, 4 * C)

    def twice(w):
        return jnp.concatenate(
            [jnp.concatenate([w, zero], axis=1), jnp.concatenate([zero, w], axis=1)], axis=0
        )

    return (grid(fwd), down, down.T, up, up.T, twice(w_out), twice(w_out.T)), grid(back)


def per_device(encoder_features, noise, patch_cols, timesteps, w_conv, w_down, w_up, w_out):
    block_cols = encoder_features.shape[1]
    lon_index = lax.axis_index("lon")
    starts_all = patch_cols[0]
    band_patches = starts_all.shape[0]

    both = jnp.stack([pack_rows(encoder_features), pack_rows(noise)])
    nxt = shifted(both, "lon", -1)
    window = jnp.concatenate([both, nxt], axis=1)

    mine = (starts_all // block_cols) == lon_index
    rank = jnp.cumsum(mine.astype(jnp.int32)) - 1
    pick = mine[None, :] & (rank[None, :] == jnp.arange(PMAX, dtype=jnp.int32)[:, None])
    starts = jnp.sum(jnp.where(pick, starts_all[None, :] - lon_index * block_cols, 0), axis=1)
    levels = jnp.sum(jnp.where(pick, timesteps[0][None, :], 0), axis=1)
    count = jnp.sum(mine.astype(jnp.int32)).reshape(1)
    sigma = sigma_of(levels)
    alphas = 1.0 / jnp.sqrt(1.0 + sigma * sigma)
    betas = alphas * sigma

    weights, w_back = layout_weights(w_conv, w_down, w_up, w_out)
    dpre, grads = run_patches(count, starts, alphas, betas, window[0], window[1], weights)

    chunks = lax.all_to_all(grads.reshape(NDEV, CHUNK, C), ("lat", "lon"), 0, 0, tiled=True)
    grad_win = run_inputs(count, starts, alphas, dpre, w_back)
    returned = shifted(grad_win[block_cols:].astype(bf16), "lon", 1)
    feature_grad = unpack_rows(grad_win[:block_cols] + returned.astype(f32))

    mean = jnp.sum(chunks.astype(f32), axis=0)
    high = mean.astype(bf16)
    total = mean[0:2].sum(axis=0)
    total_high = total.astype(bf16)
    total_low = (total - total_high.astype(f32)).astype(bf16)
    device = lax.axis_index("lat") * lax.axis_size("lon") + lon_index
    fixed = jnp.concatenate([total_high[None], total_low[None], high[2:]], axis=0)
    high = jnp.where(device == 26 * C // CHUNK, fixed, high)
    sums = lax.all_to_all(
        jnp.broadcast_to(high[None], (NDEV, CHUNK, C)), ("lat", "lon"), 0, 0, tiled=True
    ).reshape(NDEV * CHUNK, C)

    grad_conv = sums[: 9 * C].astype(f32)
    grad_down = (
        sums[9 * C : 17 * C].astype(f32).reshape(4, 2, C, C).transpose(0, 2, 1, 3).reshape(4 * C, 2 * C)
    )
    grad_up = (
        sums[17 * C : 25 * C].astype(f32).reshape(4, 2, C, C).transpose(1, 2, 0, 3).reshape(2 * C, 4 * C)
    )
    grad_out = sums[25 * C : 26 * C].astype(f32)
    objective = jnp.sum(sums[26 * C : 26 * C + 2].astype(f32)) / (2.0 * C)
    side = encoder_features.shape[0]
    loss_value = objective / (lax.axis_size("lat") * band_patches * side * side)
    return (feature_grad, grad_conv, grad_down, grad_up, grad_out, loss_value)


def solution(mesh):
    placed = (
        P("lat", "lon", None),
        P("lat", "lon", None),
        P("lat", None),
        P("lat", None),
        P(),
        P(),
        P(),
        P(),
    )
    return jax.shard_map(
        per_device,
        mesh=mesh,
        in_specs=placed,
        out_specs=(P("lat", "lon", None), P(), P(), P(), P(), P()),
        check_vma=False,
    )
```

```python
import math

import jax
import jax.numpy as jnp
from jax import lax
from jax.experimental import pallas as pl
from jax.experimental.pallas import tpu as pltpu
from jax.sharding import PartitionSpec as P

NSTEPS = 32
PMAX = 12
SIDE = 32
HALF = 16
C = 128
CELLS = SIDE * HALF
CHUNK = 32
NCHIP = 64
BLOCKS = 16

sigma_low = 0.02
sigma_high = 20.0

bf16 = jnp.bfloat16
f32 = jnp.float32


LON = ("x", "core")
CHIPS = ("lat", "x")


def shifted(block, axis, distance):
    size = lax.axis_size(axis)
    route = [((i - distance) % size, i) for i in range(size)]
    return lax.ppermute(block, axis, route)


def sigma_of(levels):
    return sigma_low * jnp.exp(
        levels.astype(jnp.float32) / (NSTEPS - 1) * math.log(sigma_high / sigma_low)
    )


def dot(a, b):
    return jnp.dot(a, b, preferred_element_type=f32)


def dot_t(a, b):
    return lax.dot_general(a, b, (((0,), (0,)), ((), ())), preferred_element_type=f32)


def pack_rows(block):
    rows, cols, chans = block.shape
    return block.reshape(rows // 2, 2, cols, chans).transpose(2, 0, 1, 3).reshape(
        cols, rows // 2, 2 * chans
    )


def unpack_rows(block):
    cols, half, lanes = block.shape
    return block.reshape(cols, half, 2, lanes // 2).transpose(1, 2, 0, 3).reshape(
        2 * half, cols, lanes // 2
    )


def fill_slots(slots, value):
    row = lax.broadcasted_iota(jnp.int32, (CELLS, C), 0) % HALF
    even = value[:, :C]
    odd = value[:, C:]
    above = jnp.where(row == 0, 0.0, pltpu.roll(odd, 1, 0))
    below = jnp.where(row == HALF - 1, 0.0, pltpu.roll(even, CELLS - 1, 0))
    slots[1 : SIDE + 1, :, 0:C] = above.astype(bf16).reshape(SIDE, HALF, C)
    slots[1 : SIDE + 1, :, C : 3 * C] = value.astype(bf16).reshape(SIDE, HALF, 2 * C)
    slots[1 : SIDE + 1, :, 3 * C : 4 * C] = below.astype(bf16).reshape(SIDE, HALF, C)


def zero_edges(slots):
    slots[0] = jnp.zeros((HALF, 4 * C), bf16)
    slots[SIDE + 1] = jnp.zeros((HALF, 4 * C), bf16)


def taps(slots):
    return jnp.concatenate(
        [slots[d : d + SIDE].reshape(CELLS, 4 * C) for d in range(3)], axis=-1
    )


def patch_kernel(
    count, parity, starts, alphas, betas,
    feat, noise, w_in, w_dn, w_dn_t, w_u, w_u_t, w_o, w_o_t,
    dpre_out, grads_out,
    slots, first, slope, g_conv, g_down, g_up, g_out, loss,
):
    g_conv[...] = jnp.zeros_like(g_conv)
    g_down[...] = jnp.zeros_like(g_down)
    g_up[...] = jnp.zeros_like(g_up)
    g_out[...] = jnp.zeros_like(g_out)
    loss[...] = jnp.zeros_like(loss)
    zero_edges(slots)

    def one_patch(k, carry):
        start = starts[k]
        f = feat[pl.ds(start, SIDE)].reshape(CELLS, 2 * C).astype(f32)
        e = noise[pl.ds(start, SIDE)].reshape(CELLS, 2 * C).astype(f32)
        fill_slots(slots, alphas[k] * f + betas[k] * e)
        pre = dot(taps(slots), w_in[...])
        sig = 0.5 * jnp.tanh(0.5 * pre) + 0.5
        act = pre * sig
        slope[...] = (sig + act * (1.0 - sig)).reshape(SLOPE)
        first[...] = act.astype(bf16).reshape(SLOPE)
        cells = jnp.concatenate([first[:, b].reshape(256, 256) for b in range(2)], axis=-1)
        pre2 = dot(cells, w_dn[...])
        sig2 = 0.5 * jnp.tanh(0.5 * pre2) + 0.5
        act2 = pre2 * sig2
        slope2 = sig2 + act2 * (1.0 - sig2)
        coarse = act2.astype(bf16)
        up = dot(coarse, w_u[...])
        ep = noise.at[pl.ds(start, SIDE)]
        merged = []
        dmerged = []
        derr = []
        for b in range(2):
            m = (first[:, b].reshape(256, 256).astype(f32) + up[:, 256 * b : 256 * b + 256]).astype(bf16)
            eps = ep[...].reshape(HALF, 2, HALF, 2 * C)[:, b].reshape(256, 256).astype(f32)
            err = dot(m, w_o[...]) - eps
            loss[...] += jnp.sum((err * err).reshape(32, 8, 256), axis=0)
            d = (err * (1.0 / C)).astype(bf16)
            merged.append(m)
            derr.append(d)
            dmerged.append(dot(d, w_o_t[...]).astype(bf16))
        g_out[...] += dot_t(jnp.concatenate(merged, axis=0), jnp.concatenate(derr, axis=0))
        dm = jnp.concatenate(dmerged, axis=-1)
        g_up[...] += dot_t(coarse, dm)
        dpre2 = (dot(dm, w_u_t[...]) * slope2).astype(bf16)
        g_down[...] += dot_t(dpre2, cells)
        dcells = dot(dpre2, w_dn_t[...])
        for b in range(2):
            df = dmerged[b].astype(f32) + dcells[:, 256 * b : 256 * b + 256]
            dp = df * slope[:, b].reshape(256, 256)
            first[:, b] = dp.astype(bf16).reshape(HALF, HALF, 2 * C)
        dpre = first[...].reshape(CELLS, 2 * C)
        dpre_out[k] = dpre
        g_conv[...] += dot_t(dpre, taps(slots))
        return carry

    lax.fori_loop(0, count[0], one_patch, 0)

    def put(index, block):
        half = index // BLOCKS
        grads_out[half ^ parity[0], pl.ds(index % BLOCKS * C, C)] = block.astype(bf16)

    for i in range(3):
        for j in range(3):
            block = g_conv[0:C, pl.ds((4 * j + i) * C, C)] + g_conv[C:, pl.ds((4 * j + i + 1) * C, C)]
            put(3 * i + j, block.T)
    for a in range(2):
        for b in range(2):
            for h in range(2):
                lanes = pl.ds((2 * b + a) * C, C)
                put(9 + (2 * a + b) * 2 + h, g_down[h * C : h * C + C, lanes].T)
                put(17 + (2 * a + b) * 2 + h, g_up[h * C : h * C + C, lanes])
    put(25, g_out[0:C, 0:C] + g_out[C:, C:])
    part = loss[:, 0:C] + loss[:, C:]
    put(26, jnp.concatenate([part, jnp.zeros((C - 8, C), f32)], axis=0))
    for index in range(27, 2 * BLOCKS):
        put(index, jnp.zeros((C, C), f32))


SLOPE = (HALF, 2, HALF, 2 * C)


def input_kernel(count, starts, alphas, dpre, w_back, out, slots):
    out[...] = jnp.zeros_like(out)
    zero_edges(slots)

    def one_patch(k, carry):
        fill_slots(slots, dpre[k].astype(f32))
        back = dot(taps(slots), w_back[...]) * alphas[k]
        window = out.at[pl.ds(starts[k], SIDE)]
        window[...] += back.reshape(SIDE, HALF, 2 * C)
        return carry

    lax.fori_loop(0, count[0], one_patch, 0)


def smem():
    return pl.BlockSpec(memory_space=pltpu.SMEM)


def vmem():
    return pl.BlockSpec(memory_space=pltpu.VMEM)


def run_patches(count, parity, starts, alphas, betas, feat, noise, weights):
    return pl.pallas_call(
        patch_kernel,
        out_shape=(
            jax.ShapeDtypeStruct((PMAX, CELLS, 2 * C), bf16),
            jax.ShapeDtypeStruct((2, BLOCKS * C, C), bf16),
        ),
        in_specs=[smem()] * 5 + [vmem()] * 9,
        out_specs=(vmem(), vmem()),
        scratch_shapes=[
            pltpu.VMEM((SIDE + 2, HALF, 4 * C), bf16),
            pltpu.VMEM(SLOPE, bf16),
            pltpu.VMEM(SLOPE, f32),
            pltpu.VMEM((2 * C, 12 * C), f32),
            pltpu.VMEM((2 * C, 4 * C), f32),
            pltpu.VMEM((2 * C, 4 * C), f32),
            pltpu.VMEM((2 * C, 2 * C), f32),
            pltpu.VMEM((8, 2 * C), f32),
        ],
        compiler_params=pltpu.CompilerParams(vmem_limit_bytes=50 << 20),
        name="patches",
    )(count, parity, starts, alphas, betas, feat, noise, *weights)


def run_inputs(count, starts, alphas, dpre, w_back):
    return pl.pallas_call(
        input_kernel,
        out_shape=jax.ShapeDtypeStruct((2 * SIDE, HALF, 2 * C), f32),
        in_specs=[smem()] * 3 + [vmem()] * 2,
        out_specs=vmem(),
        scratch_shapes=[pltpu.VMEM((SIDE + 2, HALF, 4 * C), bf16)],
        compiler_params=pltpu.CompilerParams(vmem_limit_bytes=50 << 20),
        name="inputs",
    )(count, starts, alphas, dpre, w_back)


def run_finish(parity, half, other, cells):
    def finish_kernel(parity, mine, theirs, conv, down, up, out, loss):
        def write(low, high):
            def get(index):
                ref = (low, high)[index // BLOCKS]
                return ref[pl.ds(index % BLOCKS * C, C)].astype(f32)

            for index in range(9):
                conv[pl.ds(index * C, C)] = get(index)
            for q in range(4):
                for h in range(2):
                    down[pl.ds(q * C, C), pl.ds(h * C, C)] = get(9 + 2 * q + h)
                    up[pl.ds(h * C, C), pl.ds(q * C, C)] = get(17 + 2 * q + h)
            out[...] = get(25)
            loss[0] = jnp.sum(get(26)[0:8]) * (0.5 / (C * cells))

        pl.when(parity[0] == 0)(lambda: write(mine, theirs))
        pl.when(parity[0] == 1)(lambda: write(theirs, mine))

    return pl.pallas_call(
        finish_kernel,
        out_shape=(
            jax.ShapeDtypeStruct((9 * C, C), f32),
            jax.ShapeDtypeStruct((4 * C, 2 * C), f32),
            jax.ShapeDtypeStruct((2 * C, 4 * C), f32),
            jax.ShapeDtypeStruct((C, C), f32),
            jax.ShapeDtypeStruct((1,), f32),
        ),
        in_specs=[smem(), vmem(), vmem()],
        out_specs=(vmem(), vmem(), vmem(), vmem(), smem()),
        name="finish",
    )(parity, half, other)


def layout_weights(w_conv, w_down, w_up, w_out):
    zero = jnp.zeros((C, C), bf16)
    conv = w_conv.reshape(3, 3, C, C)

    def fwd(dc, s, a):
        return conv[s - a, dc] if 0 <= s - a < 3 else zero

    def back(dc, s, p):
        return conv[p + 2 - s, 2 - dc].T if 0 <= p + 2 - s < 3 else zero

    def grid(block):
        return jnp.concatenate(
            [
                jnp.concatenate([block(dc, s, a) for a in range(2)], axis=1)
                for dc in range(3)
                for s in range(4)
            ],
            axis=0,
        )

    down = w_down.reshape(2, 2, C, 2 * C).transpose(1, 0, 2, 3).reshape(4 * C, 2 * C)
    up = w_up.reshape(2 * C, 2, 2, C).transpose(0, 2, 1, 3).reshape(2 * C, 4 * C)

    def twice(w):
        return jnp.concatenate(
            [jnp.concatenate([w, zero], axis=1), jnp.concatenate([zero, w], axis=1)], axis=0
        )

    return (grid(fwd), down, down.T, up, up.T, twice(w_out), twice(w_out.T)), grid(back)


def per_device(encoder_features, noise, patch_cols, timesteps, w_conv, w_down, w_up, w_out):
    block_cols = encoder_features.shape[1]
    lon_index = lax.axis_index(LON)
    starts_all = patch_cols[0]
    band_patches = starts_all.shape[0]

    both = jnp.stack([pack_rows(encoder_features), pack_rows(noise)])
    nxt = shifted(both, LON, -1)
    window = jnp.concatenate([both, nxt], axis=1)

    mine = (starts_all // block_cols) == lon_index
    rank = jnp.cumsum(mine.astype(jnp.int32)) - 1
    pick = mine[None, :] & (rank[None, :] == jnp.arange(PMAX, dtype=jnp.int32)[:, None])
    starts = jnp.sum(jnp.where(pick, starts_all[None, :] - lon_index * block_cols, 0), axis=1)
    levels = jnp.sum(jnp.where(pick, timesteps[0][None, :], 0), axis=1)
    count = jnp.sum(mine.astype(jnp.int32)).reshape(1)
    parity = lax.axis_index("core").reshape(1)
    sigma = sigma_of(levels)
    alphas = 1.0 / jnp.sqrt(1.0 + sigma * sigma)
    betas = alphas * sigma

    weights, w_back = layout_weights(w_conv, w_down, w_up, w_out)
    dpre, grads = run_patches(count, parity, starts, alphas, betas, window[0], window[1], weights)

    theirs = shifted(grads[1], "core", 1)
    chip = (grads[0].astype(f32) + theirs.astype(f32)).astype(bf16)
    chunks = lax.all_to_all(chip.reshape(NCHIP, CHUNK, C), CHIPS, 0, 0, tiled=True)
    grad_win = run_inputs(count, starts, alphas, dpre, w_back)
    returned = shifted(grad_win[block_cols:].astype(bf16), LON, 1)
    feature_grad = unpack_rows(grad_win[:block_cols] + returned.astype(f32))

    total = jnp.sum(chunks.astype(f32), axis=0).astype(bf16)
    half = lax.all_to_all(
        jnp.broadcast_to(total[None], (NCHIP, CHUNK, C)), CHIPS, 0, 0, tiled=True
    ).reshape(BLOCKS * C, C)
    other = shifted(half, "core", 1)
    cells = lax.axis_size("lat") * band_patches * encoder_features.shape[0] ** 2
    grad_conv, grad_down, grad_up, grad_out, loss = run_finish(parity, half, other, cells)
    return (feature_grad, grad_conv, grad_down, grad_up, grad_out, loss.reshape(()))


def solution(mesh):
    lats, lons = mesh.devices.shape
    chips = jax.sharding.Mesh(mesh.devices.reshape(lats, lons // 2, 2), ("lat", "x", "core"))
    field = P("lat", LON, None)
    return jax.shard_map(
        per_device,
        mesh=chips,
        in_specs=(field, field, P("lat", None), P("lat", None), P(), P(), P(), P()),
        out_specs=(field, P(), P(), P(), P(), P()),
        check_vma=False,
    )
```

```python
import math

import jax
import jax.numpy as jnp
from jax import lax
from jax.experimental import pallas as pl
from jax.experimental.pallas import tpu as pltpu
from jax.sharding import PartitionSpec as P

NSTEPS = 32
PMAX = 12
SIDE = 32
HALF = 16
C = 128
CELLS = SIDE * HALF
CHUNK = 32
NCHIP = 64
BLOCKS = 16

sigma_low = 0.02
sigma_high = 20.0

bf16 = jnp.bfloat16
f32 = jnp.float32


LON = ("x", "core")
CHIPS = ("lat", "x")


def shifted(block, axis, distance):
    size = lax.axis_size(axis)
    route = [((i - distance) % size, i) for i in range(size)]
    return lax.ppermute(block, axis, route)


def sigma_of(levels):
    return sigma_low * jnp.exp(
        levels.astype(jnp.float32) / (NSTEPS - 1) * math.log(sigma_high / sigma_low)
    )


def dot(a, b):
    return jnp.dot(a, b, preferred_element_type=f32)


def dot_t(a, b):
    return lax.dot_general(a, b, (((0,), (0,)), ((), ())), preferred_element_type=f32)


def pack_rows(block):
    rows, cols, chans = block.shape
    return block.reshape(rows // 2, 2, cols, chans).transpose(2, 0, 1, 3).reshape(
        cols, rows // 2, 2 * chans
    )


def unpack_rows(block):
    cols, half, lanes = block.shape
    return block.reshape(cols, half, 2, lanes // 2).transpose(1, 2, 0, 3).reshape(
        2 * half, cols, lanes // 2
    )


def fill_slots(slots, value):
    row = lax.broadcasted_iota(jnp.int32, (CELLS, C), 0) % HALF
    even = value[:, :C]
    odd = value[:, C:]
    above = jnp.where(row == 0, 0.0, pltpu.roll(odd, 1, 0))
    below = jnp.where(row == HALF - 1, 0.0, pltpu.roll(even, CELLS - 1, 0))
    slots[1 : SIDE + 1, :, 0:C] = above.astype(bf16).reshape(SIDE, HALF, C)
    slots[1 : SIDE + 1, :, C : 3 * C] = value.astype(bf16).reshape(SIDE, HALF, 2 * C)
    slots[1 : SIDE + 1, :, 3 * C : 4 * C] = below.astype(bf16).reshape(SIDE, HALF, C)


def zero_edges(slots):
    slots[0] = jnp.zeros((HALF, 4 * C), bf16)
    slots[SIDE + 1] = jnp.zeros((HALF, 4 * C), bf16)


def taps(slots):
    return jnp.concatenate(
        [slots[d : d + SIDE].reshape(CELLS, 4 * C) for d in range(3)], axis=-1
    )


def patch_kernel(
    count, parity, starts, alphas, betas,
    feat, noise, w_in, w_dn, w_dn_t, w_u, w_u_t, w_o, w_o_t,
    dpre_out, grads_out,
    slots, first, slope, g_conv, g_down, g_up, g_out, loss,
):
    g_conv[...] = jnp.zeros_like(g_conv)
    g_down[...] = jnp.zeros_like(g_down)
    g_up[...] = jnp.zeros_like(g_up)
    g_out[...] = jnp.zeros_like(g_out)
    loss[...] = jnp.zeros_like(loss)
    zero_edges(slots)

    def one_patch(k, carry):
        start = starts[k]
        f = feat[pl.ds(start, SIDE)].reshape(CELLS, 2 * C).astype(f32)
        e = noise[pl.ds(start, SIDE)].reshape(CELLS, 2 * C).astype(f32)
        fill_slots(slots, alphas[k] * f + betas[k] * e)
        pre = dot(taps(slots), w_in[...])
        sig = 0.5 * jnp.tanh(0.5 * pre) + 0.5
        act = pre * sig
        slope[...] = (sig + act * (1.0 - sig)).reshape(SLOPE)
        first[...] = act.astype(bf16).reshape(SLOPE)
        cells = jnp.concatenate([first[:, b].reshape(256, 256) for b in range(2)], axis=-1)
        pre2 = dot(cells, w_dn[...])
        sig2 = 0.5 * jnp.tanh(0.5 * pre2) + 0.5
        act2 = pre2 * sig2
        slope2 = sig2 + act2 * (1.0 - sig2)
        coarse = act2.astype(bf16)
        up = dot(coarse, w_u[...])
        ep = noise.at[pl.ds(start, SIDE)]
        merged = []
        dmerged = []
        derr = []
        for b in range(2):
            m = (first[:, b].reshape(256, 256).astype(f32) + up[:, 256 * b : 256 * b + 256]).astype(bf16)
            eps = ep[...].reshape(HALF, 2, HALF, 2 * C)[:, b].reshape(256, 256).astype(f32)
            err = dot(m, w_o[...]) - eps
            loss[...] += jnp.sum((err * err).reshape(32, 8, 256), axis=0)
            d = (err * (1.0 / C)).astype(bf16)
            merged.append(m)
            derr.append(d)
            dmerged.append(dot(d, w_o_t[...]).astype(bf16))
        g_out[...] += dot_t(jnp.concatenate(merged, axis=0), jnp.concatenate(derr, axis=0))
        dm = jnp.concatenate(dmerged, axis=-1)
        g_up[...] += dot_t(coarse, dm)
        dpre2 = (dot(dm, w_u_t[...]) * slope2).astype(bf16)
        g_down[...] += dot_t(dpre2, cells)
        dcells = dot(dpre2, w_dn_t[...])
        for b in range(2):
            df = dmerged[b].astype(f32) + dcells[:, 256 * b : 256 * b + 256]
            dp = df * slope[:, b].reshape(256, 256)
            first[:, b] = dp.astype(bf16).reshape(HALF, HALF, 2 * C)
        dpre = first[...].reshape(CELLS, 2 * C)
        dpre_out[k] = dpre
        g_conv[...] += dot_t(dpre, taps(slots))
        return carry

    lax.fori_loop(0, count[0], one_patch, 0)

    def put(index, block):
        half = index // BLOCKS
        grads_out[half ^ parity[0], pl.ds(index % BLOCKS * C, C)] = block.astype(bf16)

    for i in range(3):
        for j in range(3):
            block = g_conv[0:C, pl.ds((4 * j + i) * C, C)] + g_conv[C:, pl.ds((4 * j + i + 1) * C, C)]
            put(3 * i + j, block.T)
    for a in range(2):
        for b in range(2):
            for h in range(2):
                lanes = pl.ds((2 * b + a) * C, C)
                put(9 + (2 * a + b) * 2 + h, g_down[h * C : h * C + C, lanes].T)
                put(17 + (2 * a + b) * 2 + h, g_up[h * C : h * C + C, lanes])
    put(25, g_out[0:C, 0:C] + g_out[C:, C:])
    part = loss[:, 0:C] + loss[:, C:]
    put(26, jnp.concatenate([part, jnp.zeros((C - 8, C), f32)], axis=0))
    for index in range(27, 2 * BLOCKS):
        put(index, jnp.zeros((C, C), f32))


SLOPE = (HALF, 2, HALF, 2 * C)


def input_kernel(count, starts, alphas, dpre, w_back, out, slots):
    out[...] = jnp.zeros_like(out)
    zero_edges(slots)

    def one_patch(k, carry):
        fill_slots(slots, dpre[k].astype(f32))
        back = dot(taps(slots), w_back[...]) * alphas[k]
        window = out.at[pl.ds(starts[k], SIDE)]
        window[...] += back.reshape(SIDE, HALF, 2 * C)
        return carry

    lax.fori_loop(0, count[0], one_patch, 0)


def smem():
    return pl.BlockSpec(memory_space=pltpu.SMEM)


def vmem():
    return pl.BlockSpec(memory_space=pltpu.VMEM)


def run_patches(count, parity, starts, alphas, betas, feat, noise, weights):
    return pl.pallas_call(
        patch_kernel,
        out_shape=(
            jax.ShapeDtypeStruct((PMAX, CELLS, 2 * C), bf16),
            jax.ShapeDtypeStruct((2, BLOCKS * C, C), bf16),
        ),
        in_specs=[smem()] * 5 + [vmem()] * 9,
        out_specs=(vmem(), vmem()),
        scratch_shapes=[
            pltpu.VMEM((SIDE + 2, HALF, 4 * C), bf16),
            pltpu.VMEM(SLOPE, bf16),
            pltpu.VMEM(SLOPE, f32),
            pltpu.VMEM((2 * C, 12 * C), f32),
            pltpu.VMEM((2 * C, 4 * C), f32),
            pltpu.VMEM((2 * C, 4 * C), f32),
            pltpu.VMEM((2 * C, 2 * C), f32),
            pltpu.VMEM((8, 2 * C), f32),
        ],
        compiler_params=pltpu.CompilerParams(vmem_limit_bytes=50 << 20),
        name="patches",
    )(count, parity, starts, alphas, betas, feat, noise, *weights)


def run_inputs(count, starts, alphas, dpre, w_back):
    return pl.pallas_call(
        input_kernel,
        out_shape=jax.ShapeDtypeStruct((2 * SIDE, HALF, 2 * C), f32),
        in_specs=[smem()] * 3 + [vmem()] * 2,
        out_specs=vmem(),
        scratch_shapes=[pltpu.VMEM((SIDE + 2, HALF, 4 * C), bf16)],
        compiler_params=pltpu.CompilerParams(vmem_limit_bytes=50 << 20),
        name="inputs",
    )(count, starts, alphas, dpre, w_back)


def run_finish(parity, half, other, cells):
    def finish_kernel(parity, mine, theirs, conv, down, up, out, loss):
        def write(low, high):
            def get(index):
                ref = (low, high)[index // BLOCKS]
                return ref[pl.ds(index % BLOCKS * C, C)].astype(f32)

            for index in range(9):
                conv[pl.ds(index * C, C)] = get(index)
            for q in range(4):
                for h in range(2):
                    down[pl.ds(q * C, C), pl.ds(h * C, C)] = get(9 + 2 * q + h)
                    up[pl.ds(h * C, C), pl.ds(q * C, C)] = get(17 + 2 * q + h)
            out[...] = get(25)
            loss[0] = jnp.sum(get(26)[0:8]) * (0.5 / (C * cells))

        pl.when(parity[0] == 0)(lambda: write(mine, theirs))
        pl.when(parity[0] == 1)(lambda: write(theirs, mine))

    return pl.pallas_call(
        finish_kernel,
        out_shape=(
            jax.ShapeDtypeStruct((9 * C, C), f32),
            jax.ShapeDtypeStruct((4 * C, 2 * C), f32),
            jax.ShapeDtypeStruct((2 * C, 4 * C), f32),
            jax.ShapeDtypeStruct((C, C), f32),
            jax.ShapeDtypeStruct((1,), f32),
        ),
        in_specs=[smem(), vmem(), vmem()],
        out_specs=(vmem(), vmem(), vmem(), vmem(), smem()),
        name="finish",
    )(parity, half, other)


def layout_weights(w_conv, w_down, w_up, w_out):
    zero = jnp.zeros((C, C), bf16)
    conv = w_conv.reshape(3, 3, C, C)

    def fwd(dc, s, a):
        return conv[s - a, dc] if 0 <= s - a < 3 else zero

    def back(dc, s, p):
        return conv[p + 2 - s, 2 - dc].T if 0 <= p + 2 - s < 3 else zero

    def grid(block):
        return jnp.concatenate(
            [
                jnp.concatenate([block(dc, s, a) for a in range(2)], axis=1)
                for dc in range(3)
                for s in range(4)
            ],
            axis=0,
        )

    down = w_down.reshape(2, 2, C, 2 * C).transpose(1, 0, 2, 3).reshape(4 * C, 2 * C)
    up = w_up.reshape(2 * C, 2, 2, C).transpose(0, 2, 1, 3).reshape(2 * C, 4 * C)

    def twice(w):
        return jnp.concatenate(
            [jnp.concatenate([w, zero], axis=1), jnp.concatenate([zero, w], axis=1)], axis=0
        )

    return (grid(fwd), down, down.T, up, up.T, twice(w_out), twice(w_out.T)), grid(back)


def per_device(encoder_features, noise, patch_cols, timesteps, w_conv, w_down, w_up, w_out):
    block_cols = encoder_features.shape[1]
    lon_index = lax.axis_index(LON)
    starts_all = patch_cols[0]
    band_patches = starts_all.shape[0]

    both = jnp.stack([pack_rows(encoder_features), pack_rows(noise)])
    nxt = shifted(both, LON, -1)
    window = jnp.concatenate([both, nxt], axis=1)

    mine = (starts_all // block_cols) == lon_index
    rank = jnp.cumsum(mine.astype(jnp.int32)) - 1
    pick = mine[None, :] & (rank[None, :] == jnp.arange(PMAX, dtype=jnp.int32)[:, None])
    starts = jnp.sum(jnp.where(pick, starts_all[None, :] - lon_index * block_cols, 0), axis=1)
    levels = jnp.sum(jnp.where(pick, timesteps[0][None, :], 0), axis=1)
    count = jnp.sum(mine.astype(jnp.int32)).reshape(1)
    parity = lax.axis_index("core").reshape(1)
    sigma = sigma_of(levels)
    alphas = 1.0 / jnp.sqrt(1.0 + sigma * sigma)
    betas = alphas * sigma

    weights, w_back = layout_weights(w_conv, w_down, w_up, w_out)
    dpre, grads = run_patches(count, parity, starts, alphas, betas, window[0], window[1], weights)

    theirs = shifted(grads[1], "core", 1)
    chip = (grads[0].astype(f32) + theirs.astype(f32)).astype(bf16)
    chip, dpre = lax.optimization_barrier((chip, dpre))
    chunks = lax.all_to_all(chip.reshape(NCHIP, CHUNK, C), CHIPS, 0, 0, tiled=True)
    grad_win = run_inputs(count, starts, alphas, dpre, w_back)
    chunks, grad_win = lax.optimization_barrier((chunks, grad_win))
    returned = shifted(grad_win[block_cols:].astype(bf16), LON, 1)
    feature_grad = unpack_rows(grad_win[:block_cols] + returned.astype(f32))

    total = jnp.sum(chunks.astype(f32), axis=0).astype(bf16)
    half = lax.all_to_all(
        jnp.broadcast_to(total[None], (NCHIP, CHUNK, C)), CHIPS, 0, 0, tiled=True
    ).reshape(BLOCKS * C, C)
    half, feature_grad = lax.optimization_barrier((half, feature_grad))
    other = shifted(half, "core", 1)
    cells = lax.axis_size("lat") * band_patches * encoder_features.shape[0] ** 2
    grad_conv, grad_down, grad_up, grad_out, loss = run_finish(parity, half, other, cells)
    return (feature_grad, grad_conv, grad_down, grad_up, grad_out, loss.reshape(()))


def solution(mesh):
    lats, lons = mesh.devices.shape
    chips = jax.sharding.Mesh(mesh.devices.reshape(lats, lons // 2, 2), ("lat", "x", "core"))
    field = P("lat", LON, None)
    return jax.shard_map(
        per_device,
        mesh=chips,
        in_specs=(field, field, P("lat", None), P("lat", None), P(), P(), P(), P()),
        out_specs=(field, P(), P(), P(), P(), P()),
        check_vma=False,
    )
```

```python
import math

import jax
import jax.numpy as jnp
from jax import lax
from jax.experimental import pallas as pl
from jax.experimental.pallas import tpu as pltpu
from jax.sharding import PartitionSpec as P

NSTEPS = 32
PMAX = 12
SIDE = 32
HALF = 16
C = 128
CELLS = SIDE * HALF
CHUNK = 32
NCHIP = 64
BLOCKS = 16

sigma_low = 0.02
sigma_high = 20.0

bf16 = jnp.bfloat16
f32 = jnp.float32


LON = ("x", "core")
CHIPS = ("lat", "x")


def shifted(block, axis, distance):
    size = lax.axis_size(axis)
    route = [((i - distance) % size, i) for i in range(size)]
    return lax.ppermute(block, axis, route)


def sigma_of(levels):
    return sigma_low * jnp.exp(
        levels.astype(jnp.float32) / (NSTEPS - 1) * math.log(sigma_high / sigma_low)
    )


def dot(a, b):
    return jnp.dot(a, b, preferred_element_type=f32)


def dot_t(a, b):
    return lax.dot_general(a, b, (((0,), (0,)), ((), ())), preferred_element_type=f32)


def pack_rows(block):
    rows, cols, chans = block.shape
    return block.reshape(rows // 2, 2, cols, chans).transpose(2, 0, 1, 3).reshape(
        cols, rows // 2, 2 * chans
    )


def unpack_rows(block):
    cols, half, lanes = block.shape
    return block.reshape(cols, half, 2, lanes // 2).transpose(1, 2, 0, 3).reshape(
        2 * half, cols, lanes // 2
    )


def fill_slots(slots, value):
    row = lax.broadcasted_iota(jnp.int32, (CELLS, C), 0) % HALF
    even = value[:, :C]
    odd = value[:, C:]
    above = jnp.where(row == 0, 0.0, pltpu.roll(odd, 1, 0))
    below = jnp.where(row == HALF - 1, 0.0, pltpu.roll(even, CELLS - 1, 0))
    slots[1 : SIDE + 1, :, 0:C] = above.astype(bf16).reshape(SIDE, HALF, C)
    slots[1 : SIDE + 1, :, C : 3 * C] = value.astype(bf16).reshape(SIDE, HALF, 2 * C)
    slots[1 : SIDE + 1, :, 3 * C : 4 * C] = below.astype(bf16).reshape(SIDE, HALF, C)


def zero_edges(slots):
    slots[0] = jnp.zeros((HALF, 4 * C), bf16)
    slots[SIDE + 1] = jnp.zeros((HALF, 4 * C), bf16)


def taps(slots):
    return jnp.concatenate(
        [slots[d : d + SIDE].reshape(CELLS, 4 * C) for d in range(3)], axis=-1
    )


def patch_kernel(
    count, parity, starts, alphas, betas,
    own, right, far, w_in, w_dn, w_dn_t, w_u, w_u_t, w_o, w_o_t,
    dpre_out, keep, send,
    window, grads, slots, first, slope, g_conv, g_down, g_up, g_out, loss,
):
    g_conv[...] = jnp.zeros_like(g_conv)
    g_down[...] = jnp.zeros_like(g_down)
    g_up[...] = jnp.zeros_like(g_up)
    g_out[...] = jnp.zeros_like(g_out)
    loss[...] = jnp.zeros_like(loss)
    zero_edges(slots)
    core = parity[0]
    for block, place in ((own, core), (right, core + 1), (far, 2 - 2 * core)):
        for i in range(2):
            window[i, pl.ds(place * SIDE, SIDE)] = block[i]

    def one_patch(k, carry):
        start = starts[k]
        f = window[0, pl.ds(start, SIDE)].reshape(CELLS, 2 * C).astype(f32)
        e = window[1, pl.ds(start, SIDE)].reshape(CELLS, 2 * C).astype(f32)
        fill_slots(slots, alphas[k] * f + betas[k] * e)
        pre = dot(taps(slots), w_in[...])
        sig = 0.5 * jnp.tanh(0.5 * pre) + 0.5
        act = pre * sig
        slope[...] = (sig + act * (1.0 - sig)).reshape(SLOPE)
        first[...] = act.astype(bf16).reshape(SLOPE)
        cells = jnp.concatenate([first[:, b].reshape(256, 256) for b in range(2)], axis=-1)
        pre2 = dot(cells, w_dn[...])
        sig2 = 0.5 * jnp.tanh(0.5 * pre2) + 0.5
        act2 = pre2 * sig2
        slope2 = sig2 + act2 * (1.0 - sig2)
        coarse = act2.astype(bf16)
        up = dot(coarse, w_u[...])
        ep = window.at[1, pl.ds(start, SIDE)]
        merged = []
        dmerged = []
        derr = []
        for b in range(2):
            m = (first[:, b].reshape(256, 256).astype(f32) + up[:, 256 * b : 256 * b + 256]).astype(bf16)
            eps = ep[...].reshape(HALF, 2, HALF, 2 * C)[:, b].reshape(256, 256).astype(f32)
            err = dot(m, w_o[...]) - eps
            loss[...] += jnp.sum((err * err).reshape(32, 8, 256), axis=0)
            d = (err * (1.0 / C)).astype(bf16)
            merged.append(m)
            derr.append(d)
            dmerged.append(dot(d, w_o_t[...]).astype(bf16))
        g_out[...] += dot_t(jnp.concatenate(merged, axis=0), jnp.concatenate(derr, axis=0))
        dm = jnp.concatenate(dmerged, axis=-1)
        g_up[...] += dot_t(coarse, dm)
        dpre2 = (dot(dm, w_u_t[...]) * slope2).astype(bf16)
        g_down[...] += dot_t(dpre2, cells)
        dcells = dot(dpre2, w_dn_t[...])
        for b in range(2):
            df = dmerged[b].astype(f32) + dcells[:, 256 * b : 256 * b + 256]
            dp = df * slope[:, b].reshape(256, 256)
            first[:, b] = dp.astype(bf16).reshape(HALF, HALF, 2 * C)
        dpre = first[...].reshape(CELLS, 2 * C)
        dpre_out[k] = dpre
        g_conv[...] += dot_t(dpre, taps(slots))
        return carry

    lax.fori_loop(0, count[0], one_patch, 0)

    def put(index, block):
        half = index // BLOCKS
        grads[half ^ core, pl.ds(index % BLOCKS * C, C)] = block.astype(bf16)

    for i in range(3):
        for j in range(3):
            block = g_conv[0:C, pl.ds((4 * j + i) * C, C)] + g_conv[C:, pl.ds((4 * j + i + 1) * C, C)]
            put(3 * i + j, block.T)
    for a in range(2):
        for b in range(2):
            for h in range(2):
                lanes = pl.ds((2 * b + a) * C, C)
                put(9 + (2 * a + b) * 2 + h, g_down[h * C : h * C + C, lanes].T)
                put(17 + (2 * a + b) * 2 + h, g_up[h * C : h * C + C, lanes])
    put(25, g_out[0:C, 0:C] + g_out[C:, C:])
    part = loss[:, 0:C] + loss[:, C:]
    put(26, jnp.concatenate([part, jnp.zeros((C - 8, C), f32)], axis=0))
    for index in range(27, 2 * BLOCKS):
        put(index, jnp.zeros((C, C), f32))
    keep[...] = grads[0]
    send[...] = grads[1]


SLOPE = (HALF, 2, HALF, 2 * C)


def input_kernel(count, parity, starts, alphas, dpre, w_back, own, send, total, slots):
    total[...] = jnp.zeros_like(total)
    zero_edges(slots)

    def one_patch(k, carry):
        fill_slots(slots, dpre[k].astype(f32))
        back = dot(taps(slots), w_back[...]) * alphas[k]
        window = total.at[pl.ds(starts[k], SIDE)]
        window[...] += back.reshape(SIDE, HALF, 2 * C)
        return carry

    lax.fori_loop(0, count[0], one_patch, 0)
    own[...] = total[pl.ds(parity[0] * SIDE, SIDE)]
    send[0:SIDE] = total[pl.ds((1 - parity[0]) * SIDE, SIDE)].astype(bf16)
    send[SIDE : 2 * SIDE] = total[2 * SIDE : 3 * SIDE].astype(bf16)


def smem():
    return pl.BlockSpec(memory_space=pltpu.SMEM)


def vmem():
    return pl.BlockSpec(memory_space=pltpu.VMEM)


def run_patches(count, parity, starts, alphas, betas, blocks, weights):
    return pl.pallas_call(
        patch_kernel,
        out_shape=(
            jax.ShapeDtypeStruct((PMAX, CELLS, 2 * C), bf16),
            jax.ShapeDtypeStruct((BLOCKS * C, C), bf16),
            jax.ShapeDtypeStruct((BLOCKS * C, C), bf16),
        ),
        in_specs=[smem()] * 5 + [vmem()] * 10,
        out_specs=(vmem(), vmem(), vmem()),
        scratch_shapes=[
            pltpu.VMEM((2, 3 * SIDE, HALF, 2 * C), bf16),
            pltpu.VMEM((2, BLOCKS * C, C), bf16),
            pltpu.VMEM((SIDE + 2, HALF, 4 * C), bf16),
            pltpu.VMEM(SLOPE, bf16),
            pltpu.VMEM(SLOPE, f32),
            pltpu.VMEM((2 * C, 12 * C), f32),
            pltpu.VMEM((2 * C, 4 * C), f32),
            pltpu.VMEM((2 * C, 4 * C), f32),
            pltpu.VMEM((2 * C, 2 * C), f32),
            pltpu.VMEM((8, 2 * C), f32),
        ],
        compiler_params=pltpu.CompilerParams(vmem_limit_bytes=50 << 20),
        name="patches",
    )(count, parity, starts, alphas, betas, *blocks, *weights)


def run_inputs(count, parity, starts, alphas, dpre, w_back):
    return pl.pallas_call(
        input_kernel,
        out_shape=(
            jax.ShapeDtypeStruct((SIDE, HALF, 2 * C), f32),
            jax.ShapeDtypeStruct((2 * SIDE, HALF, 2 * C), bf16),
        ),
        in_specs=[smem()] * 4 + [vmem()] * 2,
        out_specs=(vmem(), vmem()),
        scratch_shapes=[
            pltpu.VMEM((3 * SIDE, HALF, 2 * C), f32),
            pltpu.VMEM((SIDE + 2, HALF, 4 * C), bf16),
        ],
        compiler_params=pltpu.CompilerParams(vmem_limit_bytes=50 << 20),
        name="inputs",
    )(count, parity, starts, alphas, dpre, w_back)


def run_finish(parity, half, other, cells):
    def finish_kernel(parity, mine, theirs, conv, down, up, out, loss):
        def write(low, high):
            def get(index):
                ref = (low, high)[index // BLOCKS]
                return ref[pl.ds(index % BLOCKS * C, C)].astype(f32)

            for index in range(9):
                conv[pl.ds(index * C, C)] = get(index)
            for q in range(4):
                for h in range(2):
                    down[pl.ds(q * C, C), pl.ds(h * C, C)] = get(9 + 2 * q + h)
                    up[pl.ds(h * C, C), pl.ds(q * C, C)] = get(17 + 2 * q + h)
            out[...] = get(25)
            loss[0] = jnp.sum(get(26)[0:8]) * (0.5 / (C * cells))

        pl.when(parity[0] == 0)(lambda: write(mine, theirs))
        pl.when(parity[0] == 1)(lambda: write(theirs, mine))

    return pl.pallas_call(
        finish_kernel,
        out_shape=(
            jax.ShapeDtypeStruct((9 * C, C), f32),
            jax.ShapeDtypeStruct((4 * C, 2 * C), f32),
            jax.ShapeDtypeStruct((2 * C, 4 * C), f32),
            jax.ShapeDtypeStruct((C, C), f32),
            jax.ShapeDtypeStruct((1,), f32),
        ),
        in_specs=[smem(), vmem(), vmem()],
        out_specs=(vmem(), vmem(), vmem(), vmem(), smem()),
        name="finish",
    )(parity, half, other)


def layout_weights(w_conv, w_down, w_up, w_out):
    zero = jnp.zeros((C, C), bf16)
    conv = w_conv.reshape(3, 3, C, C)

    def fwd(dc, s, a):
        return conv[s - a, dc] if 0 <= s - a < 3 else zero

    def back(dc, s, p):
        return conv[p + 2 - s, 2 - dc].T if 0 <= p + 2 - s < 3 else zero

    def grid(block):
        return jnp.concatenate(
            [
                jnp.concatenate([block(dc, s, a) for a in range(2)], axis=1)
                for dc in range(3)
                for s in range(4)
            ],
            axis=0,
        )

    down = w_down.reshape(2, 2, C, 2 * C).transpose(1, 0, 2, 3).reshape(4 * C, 2 * C)
    up = w_up.reshape(2 * C, 2, 2, C).transpose(0, 2, 1, 3).reshape(2 * C, 4 * C)

    def twice(w):
        return jnp.concatenate(
            [jnp.concatenate([w, zero], axis=1), jnp.concatenate([zero, w], axis=1)], axis=0
        )

    return (grid(fwd), down, down.T, up, up.T, twice(w_out), twice(w_out.T)), grid(back)


def per_device(encoder_features, noise, patch_cols, timesteps, w_conv, w_down, w_up, w_out):
    block_cols = encoder_features.shape[1]
    chip_index = lax.axis_index("x")
    core = lax.axis_index("core")
    starts_all = patch_cols[0]
    band_patches = starts_all.shape[0]

    both = jnp.stack([pack_rows(encoder_features), pack_rows(noise)])
    right = shifted(both, LON, -1)
    far = shifted(jnp.where(core == 0, both, right), "core", 1)

    here = (starts_all // (2 * block_cols)) == chip_index
    rank = jnp.cumsum(here.astype(jnp.int32)) - 1
    mine = here & (rank % 2 == core)
    pick = mine[None, :] & (rank[None, :] // 2 == jnp.arange(PMAX, dtype=jnp.int32)[:, None])
    starts = jnp.sum(jnp.where(pick, starts_all[None, :] - chip_index * 2 * block_cols, 0), axis=1)
    levels = jnp.sum(jnp.where(pick, timesteps[0][None, :], 0), axis=1)
    count = jnp.sum(mine.astype(jnp.int32)).reshape(1)
    parity = core.reshape(1)
    sigma = sigma_of(levels)
    alphas = 1.0 / jnp.sqrt(1.0 + sigma * sigma)
    betas = alphas * sigma

    weights, w_back = layout_weights(w_conv, w_down, w_up, w_out)
    dpre, keep, send = run_patches(
        count, parity, starts, alphas, betas, (both, right, far), weights
    )

    theirs = shifted(send, "core", 1)
    chip = (keep.astype(f32) + theirs.astype(f32)).astype(bf16)
    chip, dpre = lax.optimization_barrier((chip, dpre))
    chunks = lax.all_to_all(chip.reshape(NCHIP, CHUNK, C), CHIPS, 0, 0, tiled=True)
    own, give = run_inputs(count, parity, starts, alphas, dpre, w_back)
    taken = shifted(give, "core", 1)
    edge = (give[block_cols:].astype(f32) + taken[block_cols:].astype(f32)).astype(bf16)
    size = lax.axis_size(LON)
    returned = lax.ppermute(edge, LON, [(i, (i + 1) % size) for i in range(1, size, 2)])
    chunks, own, taken, returned = lax.optimization_barrier((chunks, own, taken, returned))
    feature_grad = unpack_rows(own + taken[:block_cols].astype(f32) + returned.astype(f32))

    total = jnp.sum(chunks.astype(f32), axis=0).astype(bf16)
    half = lax.all_to_all(
        jnp.broadcast_to(total[None], (NCHIP, CHUNK, C)), CHIPS, 0, 0, tiled=True
    ).reshape(BLOCKS * C, C)
    half, feature_grad = lax.optimization_barrier((half, feature_grad))
    other = shifted(half, "core", 1)
    cells = lax.axis_size("lat") * band_patches * encoder_features.shape[0] ** 2
    grad_conv, grad_down, grad_up, grad_out, loss = run_finish(parity, half, other, cells)
    return (feature_grad, grad_conv, grad_down, grad_up, grad_out, loss.reshape(()))


def solution(mesh):
    lats, lons = mesh.devices.shape
    chips = jax.sharding.Mesh(mesh.devices.reshape(lats, lons // 2, 2), ("lat", "x", "core"))
    field = P("lat", LON, None)
    return jax.shard_map(
        per_device,
        mesh=chips,
        in_specs=(field, field, P("lat", None), P("lat", None), P(), P(), P(), P()),
        out_specs=(field, P(), P(), P(), P(), P()),
        check_vma=False,
    )
```

```python
import math

import jax
import jax.numpy as jnp
from jax import lax
from jax.experimental import pallas as pl
from jax.experimental.pallas import tpu as pltpu
from jax.sharding import PartitionSpec as P

NSTEPS = 32
PMAX = 12
SIDE = 32
HALF = 16
C = 128
CELLS = SIDE * HALF
CHUNK = 32
NCHIP = 64
BLOCKS = 16

sigma_low = 0.02
sigma_high = 20.0

bf16 = jnp.bfloat16
f32 = jnp.float32


LON = ("x", "core")
CHIPS = ("lat", "x")


def shifted(block, axis, distance):
    size = lax.axis_size(axis)
    route = [((i - distance) % size, i) for i in range(size)]
    return lax.ppermute(block, axis, route)


def sigma_of(levels):
    return sigma_low * jnp.exp(
        levels.astype(jnp.float32) / (NSTEPS - 1) * math.log(sigma_high / sigma_low)
    )


def dot(a, b):
    return jnp.dot(a, b, preferred_element_type=f32)


def dot_t(a, b):
    return lax.dot_general(a, b, (((0,), (0,)), ((), ())), preferred_element_type=f32)


def pack_rows(block):
    rows, cols, chans = block.shape
    return block.reshape(rows // 2, 2, cols, chans).transpose(2, 0, 1, 3).reshape(
        cols, rows // 2, 2 * chans
    )


def unpack_rows(block):
    cols, half, lanes = block.shape
    return block.reshape(cols, half, 2, lanes // 2).transpose(1, 2, 0, 3).reshape(
        2 * half, cols, lanes // 2
    )


def fill_slots(slots, value):
    row = lax.broadcasted_iota(jnp.int32, (CELLS, C), 0) % HALF
    even = value[:, :C]
    odd = value[:, C:]
    above = jnp.where(row == 0, 0.0, pltpu.roll(odd, 1, 0))
    below = jnp.where(row == HALF - 1, 0.0, pltpu.roll(even, CELLS - 1, 0))
    slots[1 : SIDE + 1, :, 0:C] = above.astype(bf16).reshape(SIDE, HALF, C)
    slots[1 : SIDE + 1, :, C : 3 * C] = value.astype(bf16).reshape(SIDE, HALF, 2 * C)
    slots[1 : SIDE + 1, :, 3 * C : 4 * C] = below.astype(bf16).reshape(SIDE, HALF, C)


def zero_edges(slots):
    slots[0] = jnp.zeros((HALF, 4 * C), bf16)
    slots[SIDE + 1] = jnp.zeros((HALF, 4 * C), bf16)


def taps(slots):
    return jnp.concatenate(
        [slots[d : d + SIDE].reshape(CELLS, 4 * C) for d in range(3)], axis=-1
    )


def patch_kernel(
    count, parity, starts, alphas, betas,
    own, right, far, w_in, w_dn, w_dn_t, w_u, w_u_t, w_o, w_o_t,
    dpre_out, keep, send,
    window, grads, slots, first, slope, g_conv, g_down, g_up, g_out, loss,
):
    g_conv[...] = jnp.zeros_like(g_conv)
    g_down[...] = jnp.zeros_like(g_down)
    g_up[...] = jnp.zeros_like(g_up)
    g_out[...] = jnp.zeros_like(g_out)
    loss[...] = jnp.zeros_like(loss)
    zero_edges(slots)
    core = parity[0]
    for block, place in ((own, core), (right, core + 1), (far, 2 - 2 * core)):
        for i in range(2):
            window[i, pl.ds(place * SIDE, SIDE)] = block[i]

    def one_patch(k, carry):
        start = starts[k]
        f = window[0, pl.ds(start, SIDE)].reshape(CELLS, 2 * C).astype(f32)
        e = window[1, pl.ds(start, SIDE)].reshape(CELLS, 2 * C).astype(f32)
        fill_slots(slots, alphas[k] * f + betas[k] * e)
        pre = dot(taps(slots), w_in[...])
        sig = 0.5 * jnp.tanh(0.5 * pre) + 0.5
        act = pre * sig
        slope[...] = (sig + act * (1.0 - sig)).reshape(SLOPE)
        first[...] = act.astype(bf16).reshape(SLOPE)
        cells = jnp.concatenate([first[:, b].reshape(256, 256) for b in range(2)], axis=-1)
        pre2 = dot(cells, w_dn[...])
        sig2 = 0.5 * jnp.tanh(0.5 * pre2) + 0.5
        act2 = pre2 * sig2
        slope2 = sig2 + act2 * (1.0 - sig2)
        coarse = act2.astype(bf16)
        up = dot(coarse, w_u[...])
        ep = window.at[1, pl.ds(start, SIDE)]
        merged = []
        dmerged = []
        derr = []
        for b in range(2):
            m = (first[:, b].reshape(256, 256).astype(f32) + up[:, 256 * b : 256 * b + 256]).astype(bf16)
            eps = ep[...].reshape(HALF, 2, HALF, 2 * C)[:, b].reshape(256, 256).astype(f32)
            err = dot(m, w_o[...]) - eps
            loss[...] += jnp.sum((err * err).reshape(32, 8, 256), axis=0)
            d = (err * (1.0 / C)).astype(bf16)
            merged.append(m)
            derr.append(d)
            dmerged.append(dot(d, w_o_t[...]).astype(bf16))
        g_out[...] += dot_t(jnp.concatenate(merged, axis=0), jnp.concatenate(derr, axis=0))
        dm = jnp.concatenate(dmerged, axis=-1)
        g_up[...] += dot_t(coarse, dm)
        dpre2 = (dot(dm, w_u_t[...]) * slope2).astype(bf16)
        g_down[...] += dot_t(dpre2, cells)
        dcells = dot(dpre2, w_dn_t[...])
        for b in range(2):
            df = dmerged[b].astype(f32) + dcells[:, 256 * b : 256 * b + 256]
            dp = df * slope[:, b].reshape(256, 256)
            first[:, b] = dp.astype(bf16).reshape(HALF, HALF, 2 * C)
        dpre = first[...].reshape(CELLS, 2 * C)
        dpre_out[k] = dpre
        g_conv[...] += dot_t(dpre, taps(slots))
        return carry

    lax.fori_loop(0, count[0], one_patch, 0)

    def put(index, block):
        half = index // BLOCKS
        grads[half ^ core, pl.ds(index % BLOCKS * C, C)] = block.astype(bf16)

    for i in range(3):
        for j in range(3):
            block = g_conv[0:C, pl.ds((4 * j + i) * C, C)] + g_conv[C:, pl.ds((4 * j + i + 1) * C, C)]
            put(3 * i + j, block.T)
    for a in range(2):
        for b in range(2):
            for h in range(2):
                lanes = pl.ds((2 * b + a) * C, C)
                put(9 + (2 * a + b) * 2 + h, g_down[h * C : h * C + C, lanes].T)
                put(17 + (2 * a + b) * 2 + h, g_up[h * C : h * C + C, lanes])
    put(25, g_out[0:C, 0:C] + g_out[C:, C:])
    part = loss[:, 0:C] + loss[:, C:]
    put(26, jnp.concatenate([part, jnp.zeros((C - 8, C), f32)], axis=0))
    for index in range(27, 2 * BLOCKS):
        put(index, jnp.zeros((C, C), f32))
    keep[...] = grads[0]
    send[...] = grads[1]


SLOPE = (HALF, 2, HALF, 2 * C)


def input_kernel(count, parity, starts, alphas, dpre, w_back, own, give, edge, total, slots):
    total[...] = jnp.zeros_like(total)
    zero_edges(slots)

    def one_patch(k, carry):
        fill_slots(slots, dpre[k].astype(f32))
        back = dot(taps(slots), w_back[...]) * alphas[k]
        window = total.at[pl.ds(starts[k], SIDE)]
        window[...] += back.reshape(SIDE, HALF, 2 * C)
        return carry

    lax.fori_loop(0, count[0], one_patch, 0)
    own[...] = total[pl.ds(parity[0] * SIDE, SIDE)]
    give[...] = total[pl.ds((1 - parity[0]) * SIDE, SIDE)].astype(bf16)
    edge[...] = total[2 * SIDE : 3 * SIDE].astype(bf16)


def smem():
    return pl.BlockSpec(memory_space=pltpu.SMEM)


def vmem():
    return pl.BlockSpec(memory_space=pltpu.VMEM)


def run_patches(count, parity, starts, alphas, betas, blocks, weights):
    return pl.pallas_call(
        patch_kernel,
        out_shape=(
            jax.ShapeDtypeStruct((PMAX, CELLS, 2 * C), bf16),
            jax.ShapeDtypeStruct((BLOCKS * C, C), bf16),
            jax.ShapeDtypeStruct((BLOCKS * C, C), bf16),
        ),
        in_specs=[smem()] * 5 + [vmem()] * 10,
        out_specs=(vmem(), vmem(), vmem()),
        scratch_shapes=[
            pltpu.VMEM((2, 3 * SIDE, HALF, 2 * C), bf16),
            pltpu.VMEM((2, BLOCKS * C, C), bf16),
            pltpu.VMEM((SIDE + 2, HALF, 4 * C), bf16),
            pltpu.VMEM(SLOPE, bf16),
            pltpu.VMEM(SLOPE, f32),
            pltpu.VMEM((2 * C, 12 * C), f32),
            pltpu.VMEM((2 * C, 4 * C), f32),
            pltpu.VMEM((2 * C, 4 * C), f32),
            pltpu.VMEM((2 * C, 2 * C), f32),
            pltpu.VMEM((8, 2 * C), f32),
        ],
        compiler_params=pltpu.CompilerParams(vmem_limit_bytes=50 << 20),
        name="patches",
    )(count, parity, starts, alphas, betas, *blocks, *weights)


def run_inputs(count, parity, starts, alphas, dpre, w_back):
    return pl.pallas_call(
        input_kernel,
        out_shape=(
            jax.ShapeDtypeStruct((SIDE, HALF, 2 * C), f32),
            jax.ShapeDtypeStruct((SIDE, HALF, 2 * C), bf16),
            jax.ShapeDtypeStruct((SIDE, HALF, 2 * C), bf16),
        ),
        in_specs=[smem()] * 4 + [vmem()] * 2,
        out_specs=(vmem(), vmem(), vmem()),
        scratch_shapes=[
            pltpu.VMEM((3 * SIDE, HALF, 2 * C), f32),
            pltpu.VMEM((SIDE + 2, HALF, 4 * C), bf16),
        ],
        compiler_params=pltpu.CompilerParams(vmem_limit_bytes=50 << 20),
        name="inputs",
    )(count, parity, starts, alphas, dpre, w_back)


def run_finish(parity, half, other, cells):
    def finish_kernel(parity, mine, theirs, conv, down, up, out, loss):
        def write(low, high):
            def get(index):
                ref = (low, high)[index // BLOCKS]
                return ref[pl.ds(index % BLOCKS * C, C)].astype(f32)

            for index in range(9):
                conv[pl.ds(index * C, C)] = get(index)
            for q in range(4):
                for h in range(2):
                    down[pl.ds(q * C, C), pl.ds(h * C, C)] = get(9 + 2 * q + h)
                    up[pl.ds(h * C, C), pl.ds(q * C, C)] = get(17 + 2 * q + h)
            out[...] = get(25)
            loss[0] = jnp.sum(get(26)[0:8]) * (0.5 / (C * cells))

        pl.when(parity[0] == 0)(lambda: write(mine, theirs))
        pl.when(parity[0] == 1)(lambda: write(theirs, mine))

    return pl.pallas_call(
        finish_kernel,
        out_shape=(
            jax.ShapeDtypeStruct((9 * C, C), f32),
            jax.ShapeDtypeStruct((4 * C, 2 * C), f32),
            jax.ShapeDtypeStruct((2 * C, 4 * C), f32),
            jax.ShapeDtypeStruct((C, C), f32),
            jax.ShapeDtypeStruct((1,), f32),
        ),
        in_specs=[smem(), vmem(), vmem()],
        out_specs=(vmem(), vmem(), vmem(), vmem(), smem()),
        name="finish",
    )(parity, half, other)


def layout_weights(w_conv, w_down, w_up, w_out):
    zero = jnp.zeros((C, C), bf16)
    conv = w_conv.reshape(3, 3, C, C)

    def fwd(dc, s, a):
        return conv[s - a, dc] if 0 <= s - a < 3 else zero

    def back(dc, s, p):
        return conv[p + 2 - s, 2 - dc].T if 0 <= p + 2 - s < 3 else zero

    def grid(block):
        return jnp.concatenate(
            [
                jnp.concatenate([block(dc, s, a) for a in range(2)], axis=1)
                for dc in range(3)
                for s in range(4)
            ],
            axis=0,
        )

    down = w_down.reshape(2, 2, C, 2 * C).transpose(1, 0, 2, 3).reshape(4 * C, 2 * C)
    up = w_up.reshape(2 * C, 2, 2, C).transpose(0, 2, 1, 3).reshape(2 * C, 4 * C)

    def twice(w):
        return jnp.concatenate(
            [jnp.concatenate([w, zero], axis=1), jnp.concatenate([zero, w], axis=1)], axis=0
        )

    return (grid(fwd), down, down.T, up, up.T, twice(w_out), twice(w_out.T)), grid(back)


def per_device(encoder_features, noise, patch_cols, timesteps, w_conv, w_down, w_up, w_out):
    block_cols = encoder_features.shape[1]
    chip_index = lax.axis_index("x")
    core = lax.axis_index("core")
    starts_all = patch_cols[0]
    band_patches = starts_all.shape[0]

    both = jnp.stack([pack_rows(encoder_features), pack_rows(noise)])
    right = shifted(both, LON, -1)
    far = shifted(jnp.where(core == 0, both, right), "core", 1)

    here = (starts_all // (2 * block_cols)) == chip_index
    rank = jnp.cumsum(here.astype(jnp.int32)) - 1
    mine = here & (rank % 2 == core)
    pick = mine[None, :] & (rank[None, :] // 2 == jnp.arange(PMAX, dtype=jnp.int32)[:, None])
    starts = jnp.sum(jnp.where(pick, starts_all[None, :] - chip_index * 2 * block_cols, 0), axis=1)
    levels = jnp.sum(jnp.where(pick, timesteps[0][None, :], 0), axis=1)
    count = jnp.sum(mine.astype(jnp.int32)).reshape(1)
    parity = core.reshape(1)
    sigma = sigma_of(levels)
    alphas = 1.0 / jnp.sqrt(1.0 + sigma * sigma)
    betas = alphas * sigma

    weights, w_back = layout_weights(w_conv, w_down, w_up, w_out)
    dpre, keep, send = run_patches(
        count, parity, starts, alphas, betas, (both, right, far), weights
    )

    theirs = shifted(send, "core", 1)
    chip = (keep.astype(f32) + theirs.astype(f32)).astype(bf16)
    chip, dpre = lax.optimization_barrier((chip, dpre))
    chunks = lax.all_to_all(chip.reshape(NCHIP, CHUNK, C), CHIPS, 0, 0, tiled=True)
    own, give, edge = run_inputs(count, parity, starts, alphas, dpre, w_back)
    chunks, own, give, edge = lax.optimization_barrier((chunks, own, give, edge))
    taken = shifted(give, "core", 1)
    size = lax.axis_size(LON)
    near = lax.ppermute(edge, LON, [(i, (i + 1) % size) for i in range(1, size, 2)])
    over = lax.ppermute(edge, LON, [(i, (i + 2) % size) for i in range(0, size, 2)])
    feature_grad = unpack_rows(
        own + taken.astype(f32) + (near.astype(f32) + over.astype(f32))
    )

    total = jnp.sum(chunks.astype(f32), axis=0).astype(bf16)
    half = lax.all_to_all(
        jnp.broadcast_to(total[None], (NCHIP, CHUNK, C)), CHIPS, 0, 0, tiled=True
    ).reshape(BLOCKS * C, C)
    half, feature_grad = lax.optimization_barrier((half, feature_grad))
    other = shifted(half, "core", 1)
    cells = lax.axis_size("lat") * band_patches * encoder_features.shape[0] ** 2
    grad_conv, grad_down, grad_up, grad_out, loss = run_finish(parity, half, other, cells)
    return (feature_grad, grad_conv, grad_down, grad_up, grad_out, loss.reshape(()))


def solution(mesh):
    lats, lons = mesh.devices.shape
    chips = jax.sharding.Mesh(mesh.devices.reshape(lats, lons // 2, 2), ("lat", "x", "core"))
    field = P("lat", LON, None)
    return jax.shard_map(
        per_device,
        mesh=chips,
        in_specs=(field, field, P("lat", None), P("lat", None), P(), P(), P(), P()),
        out_specs=(field, P(), P(), P(), P(), P()),
        check_vma=False,
    )
```

```python
import math

import jax
import jax.numpy as jnp
from jax import lax
from jax.experimental import pallas as pl
from jax.experimental.pallas import tpu as pltpu
from jax.sharding import PartitionSpec as P

NSTEPS = 32
PMAX = 12
SIDE = 32
HALF = 16
C = 128
CELLS = SIDE * HALF
CHUNK = 32
NCHIP = 64
BLOCKS = 16

sigma_low = 0.02
sigma_high = 20.0

bf16 = jnp.bfloat16
f32 = jnp.float32


LON = ("x", "core")
CHIPS = ("lat", "x")


def shifted(block, axis, distance):
    size = lax.axis_size(axis)
    route = [((i - distance) % size, i) for i in range(size)]
    return lax.ppermute(block, axis, route)


def sigma_of(levels):
    return sigma_low * jnp.exp(
        levels.astype(jnp.float32) / (NSTEPS - 1) * math.log(sigma_high / sigma_low)
    )


def dot(a, b):
    return jnp.dot(a, b, preferred_element_type=f32)


def dot_t(a, b):
    return lax.dot_general(a, b, (((0,), (0,)), ((), ())), preferred_element_type=f32)


def pack_rows(block):
    rows, cols, chans = block.shape
    return block.reshape(rows // 2, 2, cols, chans).transpose(2, 0, 1, 3).reshape(
        cols, rows // 2, 2 * chans
    )


def unpack_rows(block):
    cols, half, lanes = block.shape
    return block.reshape(cols, half, 2, lanes // 2).transpose(1, 2, 0, 3).reshape(
        2 * half, cols, lanes // 2
    )


def fill_slots(slots, value):
    row = lax.broadcasted_iota(jnp.int32, (CELLS, C), 0) % HALF
    even = value[:, :C]
    odd = value[:, C:]
    above = jnp.where(row == 0, 0.0, pltpu.roll(odd, 1, 0))
    below = jnp.where(row == HALF - 1, 0.0, pltpu.roll(even, CELLS - 1, 0))
    slots[1 : SIDE + 1, :, 0:C] = above.astype(bf16).reshape(SIDE, HALF, C)
    slots[1 : SIDE + 1, :, C : 3 * C] = value.astype(bf16).reshape(SIDE, HALF, 2 * C)
    slots[1 : SIDE + 1, :, 3 * C : 4 * C] = below.astype(bf16).reshape(SIDE, HALF, C)


def zero_edges(slots):
    slots[0] = jnp.zeros((HALF, 4 * C), bf16)
    slots[SIDE + 1] = jnp.zeros((HALF, 4 * C), bf16)


def taps(slots):
    return jnp.concatenate(
        [slots[d : d + SIDE].reshape(CELLS, 4 * C) for d in range(3)], axis=-1
    )


def patch_kernel(
    count, parity, starts, alphas, betas,
    own, right, far, w_in, w_dn, w_dn_t, w_u, w_u_t, w_o, w_o_t,
    dpre_out, keep, send,
    window, grads, slots, first, slope, g_conv, g_down, g_up, g_out, loss,
):
    g_conv[...] = jnp.zeros_like(g_conv)
    g_down[...] = jnp.zeros_like(g_down)
    g_up[...] = jnp.zeros_like(g_up)
    g_out[...] = jnp.zeros_like(g_out)
    loss[...] = jnp.zeros_like(loss)
    zero_edges(slots)
    core = parity[0]
    for block, place in ((own, core), (right, core + 1), (far, 2 - 2 * core)):
        for i in range(2):
            window[i, pl.ds(place * SIDE, SIDE)] = block[i]

    def one_patch(k, carry):
        start = starts[k]
        f = window[0, pl.ds(start, SIDE)].reshape(CELLS, 2 * C).astype(f32)
        e = window[1, pl.ds(start, SIDE)].reshape(CELLS, 2 * C).astype(f32)
        fill_slots(slots, alphas[k] * f + betas[k] * e)
        pre = dot(taps(slots), w_in[...])
        sig = 0.5 * jnp.tanh(0.5 * pre) + 0.5
        act = pre * sig
        slope[...] = (sig + act * (1.0 - sig)).reshape(SLOPE)
        first[...] = act.astype(bf16).reshape(SLOPE)
        cells = jnp.concatenate([first[:, b].reshape(256, 256) for b in range(2)], axis=-1)
        pre2 = dot(cells, w_dn[...])
        sig2 = 0.5 * jnp.tanh(0.5 * pre2) + 0.5
        act2 = pre2 * sig2
        slope2 = sig2 + act2 * (1.0 - sig2)
        coarse = act2.astype(bf16)
        up = dot(coarse, w_u[...])
        ep = window.at[1, pl.ds(start, SIDE)]
        merged = []
        dmerged = []
        derr = []
        for b in range(2):
            m = (first[:, b].reshape(256, 256).astype(f32) + up[:, 256 * b : 256 * b + 256]).astype(bf16)
            eps = ep[...].reshape(HALF, 2, HALF, 2 * C)[:, b].reshape(256, 256).astype(f32)
            err = dot(m, w_o[...]) - eps
            loss[...] += jnp.sum((err * err).reshape(32, 8, 256), axis=0)
            d = (err * (1.0 / C)).astype(bf16)
            merged.append(m)
            derr.append(d)
            dmerged.append(dot(d, w_o_t[...]).astype(bf16))
        g_out[...] += dot_t(jnp.concatenate(merged, axis=0), jnp.concatenate(derr, axis=0))
        dm = jnp.concatenate(dmerged, axis=-1)
        g_up[...] += dot_t(coarse, dm)
        dpre2 = (dot(dm, w_u_t[...]) * slope2).astype(bf16)
        g_down[...] += dot_t(dpre2, cells)
        dcells = dot(dpre2, w_dn_t[...])
        for b in range(2):
            df = dmerged[b].astype(f32) + dcells[:, 256 * b : 256 * b + 256]
            dp = df * slope[:, b].reshape(256, 256)
            first[:, b] = dp.astype(bf16).reshape(HALF, HALF, 2 * C)
        dpre = first[...].reshape(CELLS, 2 * C)
        dpre_out[k] = dpre
        g_conv[...] += dot_t(dpre, taps(slots))
        return carry

    lax.fori_loop(0, count[0], one_patch, 0)

    def put(index, block):
        half = index // BLOCKS
        grads[half ^ core, pl.ds(index % BLOCKS * C, C)] = block.astype(bf16)

    for i in range(3):
        for j in range(3):
            block = g_conv[0:C, pl.ds((4 * j + i) * C, C)] + g_conv[C:, pl.ds((4 * j + i + 1) * C, C)]
            put(3 * i + j, block.T)
    for a in range(2):
        for b in range(2):
            for h in range(2):
                lanes = pl.ds((2 * b + a) * C, C)
                put(9 + (2 * a + b) * 2 + h, g_down[h * C : h * C + C, lanes].T)
                put(17 + (2 * a + b) * 2 + h, g_up[h * C : h * C + C, lanes])
    put(25, g_out[0:C, 0:C] + g_out[C:, C:])
    part = loss[:, 0:C] + loss[:, C:]
    put(26, jnp.concatenate([part, jnp.zeros((C - 8, C), f32)], axis=0))
    for index in range(27, 2 * BLOCKS):
        put(index, jnp.zeros((C, C), f32))
    keep[...] = grads[0]
    send[...] = grads[1]


SLOPE = (HALF, 2, HALF, 2 * C)


def input_kernel(count, parity, starts, alphas, dpre, w_back, own, give, edge, total, slots):
    total[...] = jnp.zeros_like(total)
    zero_edges(slots)

    def one_patch(k, carry):
        fill_slots(slots, dpre[k].astype(f32))
        back = dot(taps(slots), w_back[...]) * alphas[k]
        window = total.at[pl.ds(starts[k], SIDE)]
        window[...] += back.reshape(SIDE, HALF, 2 * C)
        return carry

    lax.fori_loop(0, count[0], one_patch, 0)
    own[...] = total[pl.ds(parity[0] * SIDE, SIDE)]
    give[...] = total[pl.ds((1 - parity[0]) * SIDE, SIDE)].astype(bf16)
    edge[...] = total[2 * SIDE : 3 * SIDE].astype(bf16)


def smem():
    return pl.BlockSpec(memory_space=pltpu.SMEM)


def vmem():
    return pl.BlockSpec(memory_space=pltpu.VMEM)


def run_patches(count, parity, starts, alphas, betas, blocks, weights):
    return pl.pallas_call(
        patch_kernel,
        out_shape=(
            jax.ShapeDtypeStruct((PMAX, CELLS, 2 * C), bf16),
            jax.ShapeDtypeStruct((BLOCKS * C, C), bf16),
            jax.ShapeDtypeStruct((BLOCKS * C, C), bf16),
        ),
        in_specs=[smem()] * 5 + [vmem()] * 10,
        out_specs=(vmem(), vmem(), vmem()),
        scratch_shapes=[
            pltpu.VMEM((2, 3 * SIDE, HALF, 2 * C), bf16),
            pltpu.VMEM((2, BLOCKS * C, C), bf16),
            pltpu.VMEM((SIDE + 2, HALF, 4 * C), bf16),
            pltpu.VMEM(SLOPE, bf16),
            pltpu.VMEM(SLOPE, f32),
            pltpu.VMEM((2 * C, 12 * C), f32),
            pltpu.VMEM((2 * C, 4 * C), f32),
            pltpu.VMEM((2 * C, 4 * C), f32),
            pltpu.VMEM((2 * C, 2 * C), f32),
            pltpu.VMEM((8, 2 * C), f32),
        ],
        compiler_params=pltpu.CompilerParams(vmem_limit_bytes=50 << 20),
        name="patches",
    )(count, parity, starts, alphas, betas, *blocks, *weights)


def run_inputs(count, parity, starts, alphas, dpre, w_back):
    return pl.pallas_call(
        input_kernel,
        out_shape=(
            jax.ShapeDtypeStruct((SIDE, HALF, 2 * C), f32),
            jax.ShapeDtypeStruct((SIDE, HALF, 2 * C), bf16),
            jax.ShapeDtypeStruct((SIDE, HALF, 2 * C), bf16),
        ),
        in_specs=[smem()] * 4 + [vmem()] * 2,
        out_specs=(vmem(), vmem(), vmem()),
        scratch_shapes=[
            pltpu.VMEM((3 * SIDE, HALF, 2 * C), f32),
            pltpu.VMEM((SIDE + 2, HALF, 4 * C), bf16),
        ],
        compiler_params=pltpu.CompilerParams(vmem_limit_bytes=50 << 20),
        name="inputs",
    )(count, parity, starts, alphas, dpre, w_back)


def run_finish(parity, half, other, cells):
    def finish_kernel(parity, mine, theirs, conv, down, up, out, loss):
        def write(low, high):
            def get(index):
                ref = (low, high)[index // BLOCKS]
                return ref[pl.ds(index % BLOCKS * C, C)].astype(f32)

            for index in range(9):
                conv[pl.ds(index * C, C)] = get(index)
            for q in range(4):
                for h in range(2):
                    down[pl.ds(q * C, C), pl.ds(h * C, C)] = get(9 + 2 * q + h)
                    up[pl.ds(h * C, C), pl.ds(q * C, C)] = get(17 + 2 * q + h)
            out[...] = get(25)
            loss[0] = jnp.sum(get(26)[0:8]) * (0.5 / (C * cells))

        pl.when(parity[0] == 0)(lambda: write(mine, theirs))
        pl.when(parity[0] == 1)(lambda: write(theirs, mine))

    return pl.pallas_call(
        finish_kernel,
        out_shape=(
            jax.ShapeDtypeStruct((9 * C, C), f32),
            jax.ShapeDtypeStruct((4 * C, 2 * C), f32),
            jax.ShapeDtypeStruct((2 * C, 4 * C), f32),
            jax.ShapeDtypeStruct((C, C), f32),
            jax.ShapeDtypeStruct((1,), f32),
        ),
        in_specs=[smem(), vmem(), vmem()],
        out_specs=(vmem(), vmem(), vmem(), vmem(), smem()),
        name="finish",
    )(parity, half, other)


def layout_weights(w_conv, w_down, w_up, w_out):
    zero = jnp.zeros((C, C), bf16)
    conv = w_conv.reshape(3, 3, C, C)

    def fwd(dc, s, a):
        return conv[s - a, dc] if 0 <= s - a < 3 else zero

    def back(dc, s, p):
        return conv[p + 2 - s, 2 - dc].T if 0 <= p + 2 - s < 3 else zero

    def grid(block):
        return jnp.concatenate(
            [
                jnp.concatenate([block(dc, s, a) for a in range(2)], axis=1)
                for dc in range(3)
                for s in range(4)
            ],
            axis=0,
        )

    down = w_down.reshape(2, 2, C, 2 * C).transpose(1, 0, 2, 3).reshape(4 * C, 2 * C)
    up = w_up.reshape(2 * C, 2, 2, C).transpose(0, 2, 1, 3).reshape(2 * C, 4 * C)

    def twice(w):
        return jnp.concatenate(
            [jnp.concatenate([w, zero], axis=1), jnp.concatenate([zero, w], axis=1)], axis=0
        )

    return (grid(fwd), down, down.T, up, up.T, twice(w_out), twice(w_out.T)), grid(back)


def per_device(encoder_features, noise, patch_cols, timesteps, w_conv, w_down, w_up, w_out):
    block_cols = encoder_features.shape[1]
    chip_index = lax.axis_index("x")
    core = lax.axis_index("core")
    starts_all = patch_cols[0]
    band_patches = starts_all.shape[0]

    both = jnp.stack([pack_rows(encoder_features), pack_rows(noise)])
    right = shifted(both, LON, -1)
    far = shifted(jnp.where(core == 0, both, right), "core", 1)

    here = (starts_all // (2 * block_cols)) == chip_index
    rank = jnp.cumsum(here.astype(jnp.int32)) - 1
    mine = here & (rank % 2 == core)
    pick = mine[None, :] & (rank[None, :] // 2 == jnp.arange(PMAX, dtype=jnp.int32)[:, None])
    starts = jnp.sum(jnp.where(pick, starts_all[None, :] - chip_index * 2 * block_cols, 0), axis=1)
    levels = jnp.sum(jnp.where(pick, timesteps[0][None, :], 0), axis=1)
    count = jnp.sum(mine.astype(jnp.int32)).reshape(1)
    parity = core.reshape(1)
    sigma = sigma_of(levels)
    alphas = 1.0 / jnp.sqrt(1.0 + sigma * sigma)
    betas = alphas * sigma

    weights, w_back = layout_weights(w_conv, w_down, w_up, w_out)
    dpre, keep, send = run_patches(
        count, parity, starts, alphas, betas, (both, right, far), weights
    )

    theirs = shifted(send, "core", 1)
    chip = (keep.astype(f32) + theirs.astype(f32)).astype(bf16)
    chip, dpre = lax.optimization_barrier((chip, dpre))
    chunks = lax.all_to_all(chip.reshape(NCHIP, CHUNK, C), CHIPS, 0, 0, tiled=True)
    own, give, edge = run_inputs(count, parity, starts, alphas, dpre, w_back)
    chunks, own = lax.optimization_barrier((chunks, own))
    taken = shifted(give, "core", 1)
    size = lax.axis_size(LON)
    near = lax.ppermute(edge, LON, [(i, (i + 1) % size) for i in range(1, size, 2)])
    over = lax.ppermute(edge, LON, [(i, (i + 2) % size) for i in range(0, size, 2)])
    feature_grad = unpack_rows(
        own + taken.astype(f32) + (near.astype(f32) + over.astype(f32))
    )

    total = jnp.sum(chunks.astype(f32), axis=0).astype(bf16)
    half = lax.all_to_all(
        jnp.broadcast_to(total[None], (NCHIP, CHUNK, C)), CHIPS, 0, 0, tiled=True
    ).reshape(BLOCKS * C, C)
    half, feature_grad = lax.optimization_barrier((half, feature_grad))
    other = shifted(half, "core", 1)
    cells = lax.axis_size("lat") * band_patches * encoder_features.shape[0] ** 2
    grad_conv, grad_down, grad_up, grad_out, loss = run_finish(parity, half, other, cells)
    return (feature_grad, grad_conv, grad_down, grad_up, grad_out, loss.reshape(()))


def solution(mesh):
    lats, lons = mesh.devices.shape
    chips = jax.sharding.Mesh(mesh.devices.reshape(lats, lons // 2, 2), ("lat", "x", "core"))
    field = P("lat", LON, None)
    return jax.shard_map(
        per_device,
        mesh=chips,
        in_specs=(field, field, P("lat", None), P("lat", None), P(), P(), P(), P()),
        out_specs=(field, P(), P(), P(), P(), P()),
        check_vma=False,
    )
```
